256 devices in a mesh: ctx: 32 (over y, z), uly: 8 (over x, core).
Axes of the slice: x: 4, y: 4, z: 8, core: 2. Of those that a mesh axis runs over, the one named last changes fastest.
Arguments:
- queries: bfloat16 [32768, 32, 128], P(('ctx', 'uly')), may hold values from -20 to 20
- keys: bfloat16 [32768, 8, 128], P(('ctx', 'uly')), may hold values from -20 to 20
- values: bfloat16 [32768, 8, 128], P(('ctx', 'uly')), may hold values from -6 to 6
- grad_out: bfloat16 [32768, 32, 128], P(('ctx', 'uly')), may hold values from -6 to 6
- doc_lengths: int32 [64], replicated, may hold values from 1 to 1024, 32768 in all
Outputs:
- grad_queries: bfloat16 [32768, 32, 128], P(('ctx', 'uly'))
- grad_keys: bfloat16 [32768, 8, 128], P(('ctx', 'uly'))
- grad_values: bfloat16 [32768, 8, 128], P(('ctx', 'uly'))
The draws below stay inside these ranges and needn't reach their ends.
Inputs may be any that keep to these rules, and one draw needn't show every extreme that they name: `doc_lengths`: positive lengths that sum to 32768; the longest document has exactly 1024 tokens.
All inputs are finite; a program needn't handle non-finite values.
Results may differ from the reference program's by a relative error of at most 0.0069.
Values may be sent and summed in bfloat16 or wider, within the bound.
A program may use at most 64 MiB of HBM per device.

```python
import math
import jax
import jax.numpy as jnp
import numpy as np
from jax import lax

H = 32
KVH = 8
HD = 128
CTX_TOK = 1024
SEQ = 32768
MAX_DOC = 1024
DOCS = 64


def draw_queries(key, part):
    fresh = jax.random.fold_in(key, 21)
    return jnp.clip(jax.random.normal(fresh, (SEQ, H, HD), jnp.float32), -5.0, 5.0).astype(jnp.bfloat16)


def draw_keys(key, part):
    fresh = jax.random.fold_in(key, 22)
    return jnp.clip(jax.random.normal(fresh, (SEQ, KVH, HD), jnp.float32), -5.0, 5.0).astype(jnp.bfloat16)


def levels(own_key, dims, pieces, low, largest):
    level = 1.0
    for axis_at, parts in pieces:
        steps = jax.random.uniform(jax.random.fold_in(jax.random.fold_in(own_key, 6), axis_at), (parts,), jnp.float32, low / len(pieces), largest / len(pieces))
        level = level * jnp.repeat(jnp.exp(steps), dims[axis_at] // parts).reshape((-1,) + (1,) * (len(dims) - 1 - axis_at))
    return level


def length_profile(number_of, total, reach, slope):
    weights = [(1 << 20) // math.isqrt(standing ** slope) + 1 for standing in range(2, number_of + 1)]
    rest, holding = total - reach - (number_of - 1), [1] * (number_of - 1)
    while rest > 0:
        free = [i for i in range(number_of - 1) if holding[i] < reach]
        whole, budget = sum([weights[i] for i in free]), rest
        for i in free:
            more = min(reach - holding[i], max(1, budget * weights[i] // whole), rest)
            holding[i] = holding[i] + more
            rest = rest - more
    return np.array([reach] + holding)


def ragged_sizes(own_key, amount, total, bound, skew):
    if amount == 2:
        one = jax.random.randint(own_key, (), max(1, total - bound), min(bound, total - 1) + 1)
        return jnp.stack([one, total - one])
    lengths = jnp.asarray(length_profile(amount, total, bound, skew), jnp.int32)
    couples = (amount - 1) // 2
    source_of, sink = lengths[1:1 + 2 * couples:2], lengths[2:2 + 2 * couples:2]
    margin = jnp.minimum(source_of - 1, bound - sink)
    shifted = jax.random.randint(jax.random.fold_in(own_key, 1), (couples,), 0, 1 << 20) % (margin + 1)
    lengths = lengths.at[1:1 + 2 * couples:2].set(source_of - shifted).at[2:2 + 2 * couples:2].set(sink + shifted)
    return lengths[jax.random.permutation(jax.random.fold_in(own_key, 2), amount)]


def bell_draw(stream_key, extent, scale, limit, cuts=(), kind=jnp.bfloat16):
    array = jax.random.normal(stream_key, extent, jnp.float32) * scale
    if len(cuts) > 0:
        array = levels(stream_key, extent, cuts, -0.22, 0.18) * array
    return jnp.clip(array, min=-limit, max=limit).astype(kind)


def setup_inputs(seed: int = 0) -> dict:
    arg_keys = jax.random.split(jax.random.key(seed), 6)
    queries = draw_queries(jax.random.fold_in(arg_keys[5], 71), 0)
    keys = draw_keys(jax.random.fold_in(arg_keys[5], 71), 0)
    values = bell_draw(arg_keys[2], (SEQ, KVH, HD), 1.0, 6.0, ((0, 256),))
    grad_out = bell_draw(arg_keys[3], (SEQ, H, HD), 1.0, 6.0, ((0, 256),))
    doc_lengths = ragged_sizes(arg_keys[4], DOCS, SEQ, MAX_DOC, 2).astype(jnp.int32)
    return {"queries": queries, "keys": keys, "values": values, "grad_out": grad_out, "doc_lengths": doc_lengths}


def doc_number(positions, doc_ends):
    return jnp.sum((positions[:, None] >= doc_ends[None, :]).astype(jnp.int32), axis=1)


def reference(queries, keys, values, grad_out, doc_lengths):
    group_size = H // KVH
    softmax_scale = HD ** -0.5
    doc_ends = jnp.cumsum(doc_lengths).astype(jnp.int32)
    window = MAX_DOC + CTX_TOK
    padding = jnp.zeros((MAX_DOC, KVH, HD), keys.dtype)
    padded_keys = jnp.concatenate([padding, keys], axis=0)
    padded_values = jnp.concatenate([padding, values], axis=0)
    grouped_query_rows = queries.reshape(SEQ, KVH, group_size, HD)
    grouped_output_gradient = grad_out.reshape(SEQ, KVH, group_size, HD)

    def per_block(carry, block_number):
        grad_k, grad_v = carry
        offset = (block_number * CTX_TOK).astype(jnp.int32)
        query_tile_rows = lax.dynamic_slice_in_dim(grouped_query_rows, offset, CTX_TOK, 0).astype(jnp.float32)
        output_gradient_block = lax.dynamic_slice_in_dim(grouped_output_gradient, offset, CTX_TOK, 0).astype(jnp.float32)
        key_tile_rows = lax.dynamic_slice_in_dim(padded_keys, offset, window, 0).astype(jnp.float32)
        value_tile_rows = lax.dynamic_slice_in_dim(padded_values, offset, window, 0).astype(jnp.float32)
        query_pos = offset + jnp.arange(CTX_TOK, dtype=jnp.int32)
        key_pos = offset - MAX_DOC + jnp.arange(window, dtype=jnp.int32)
        query_doc = doc_number(query_pos, doc_ends)
        key_doc = doc_number(key_pos, doc_ends)
        allowed = (key_doc[None, :] == query_doc[:, None]) & (key_pos[None, :] <= query_pos[:, None]) & (key_pos[None, :] >= 0)
        logit_scores = jnp.einsum("nyej,xyj->yenx", query_tile_rows, key_tile_rows) * softmax_scale
        row_max = jnp.max(jnp.where(allowed, logit_scores, -1.0e30), axis=-1)
        expo = jnp.where(allowed, jnp.exp(logit_scores - row_max[..., None]), 0.0)
        log_total = row_max + jnp.log(jnp.sum(expo, axis=-1))
        prob = jnp.where(allowed, jnp.exp(logit_scores - log_total[..., None]), 0.0)
        probability_gradient = jnp.einsum("nyej,xyj->yenx", output_gradient_block, value_tile_rows)
        delta = jnp.sum(prob * probability_gradient, axis=-1)
        dscore = prob * (probability_gradient - delta[..., None])
        probability_block = lax.optimization_barrier(prob.astype(jnp.bfloat16)).astype(jnp.float32)
        score_gradient_block = lax.optimization_barrier(dscore.astype(jnp.bfloat16)).astype(jnp.float32)
        query_gradient = (jnp.einsum("evnz,zej->nevj", score_gradient_block, key_tile_rows) * softmax_scale).astype(jnp.bfloat16)
        partial_key_gradient = jnp.einsum("etpr,peti->rei", score_gradient_block, query_tile_rows) * softmax_scale
        partial_value_gradient = jnp.einsum("etpr,peti->rei", probability_block, output_gradient_block)
        grad_k = lax.dynamic_update_slice_in_dim(grad_k, lax.dynamic_slice_in_dim(grad_k, offset, window, 0) + partial_key_gradient, offset, 0)
        grad_v = lax.dynamic_update_slice_in_dim(grad_v, lax.dynamic_slice_in_dim(grad_v, offset, window, 0) + partial_value_gradient, offset, 0)
        return (grad_k, grad_v), query_gradient

    start_k = jnp.zeros((MAX_DOC + SEQ, KVH, HD), jnp.float32)
    start_v = jnp.zeros((MAX_DOC + SEQ, KVH, HD), jnp.float32)
    (grad_k, grad_v), query_gradient = lax.scan(per_block, (start_k, start_v), jnp.arange(SEQ // CTX_TOK, dtype=jnp.int32))
    grad_queries = query_gradient.reshape(SEQ, H, HD)
    grad_keys = grad_k[MAX_DOC:].astype(jnp.bfloat16)
    grad_values = grad_v[MAX_DOC:].astype(jnp.bfloat16)
    return (grad_queries, grad_keys, grad_values)
```

```python
import jax
import jax.numpy as jnp
from jax import lax
from jax.experimental import pallas as pl
from jax.experimental.pallas import tpu as pltpu
from jax.sharding import PartitionSpec as P

MESH = pl.DeviceIdType.MESH
NT = (((1,), (1,)), ((), ()))
TN = (((0,), (0,)), ((), ()))
LOG2E = 1.4426950408889634

TOK = 128
CHIP = 256
WINDOW = 1280
SPAN = 1152
TILE = 128
ROWS = 256
PAIRS = ROWS // TOK


def kernel(
    heads,
    group,
    chips,
    blocks,
    lengths,
    q_in,
    do_in,
    kv_in,
    dq_out,
    dkv_out,
    kvb,
    qv,
    dov,
    bias,
    s_scr,
    dp_scr,
    dsb,
    acc,
    dqv,
    sbuf,
    rbuf,
    fin,
    kv_loc,
    kv_send,
    kv_recv,
    x_loc,
    x_send,
    x_recv,
    g_send,
    g_recv,
    dq_loc,
    dq_send,
    dq_recv,
    fin_loc,
    fin_send,
    fin_recv,
):
    ctx = lax.axis_index("ctx")
    uly = lax.axis_index("uly")
    x, core = uly // 2, uly % 2
    qheads = heads * group
    scale = TOK**-0.5
    chip = ctx * chips + x
    total = blocks * chips

    def at(chip_number):
        return (chip_number // chips, (chip_number % chips) * 2 + core)

    sibling = (ctx, uly + 1 - 2 * core)
    up = ((ctx + 1) % blocks, uly)
    down = ((ctx + blocks - 1) % blocks, uly)
    right = (ctx, (uly + 2) % (2 * chips))
    left = (ctx, (uly + 2 * chips - 2) % (2 * chips))
    after = at((chip + 1) % total)
    before = at((chip + total - 1) % total)
    onward = at((chip + total + 1 - 2 * core) % total)
    backward = at((chip + total - 1 + 2 * core) % total)

    pos_right = 1024 * (1 - x // (chips - 1))
    pos_left = 1024 * (1 - (x + chips - 2) // (chips - 1))
    pos_mid = 768 - 512 * core

    barrier = pltpu.get_barrier_semaphore()
    for device in (sibling, up, down, right, left, after, before):
        pl.semaphore_signal(barrier, inc=1, device_id=device, device_id_type=MESH)
    pl.semaphore_wait(barrier, 7)

    def remote(src, dst, send, recv, device):
        return pltpu.make_async_remote_copy(
            src_ref=src, dst_ref=dst, send_sem=send, recv_sem=recv, device_id=device, device_id_type=MESH
        )

    def part(h, pos):
        return kvb.at[h, :, pl.ds(pos if isinstance(pos, int) else pl.multiple_of(pos, 256), CHIP), :]

    own_rows = pl.ds(pl.multiple_of(1024 + TOK * core, TOK), TOK)
    other_rows = pl.ds(pl.multiple_of(1024 + TOK * (1 - core), TOK), TOK)

    def kv_local(h):
        return pltpu.make_async_copy(kv_in.at[heads * core + h], kvb.at[h, :, own_rows, :], kv_loc.at[h])

    def kv_swap(h, rows=own_rows):
        return remote(kv_in.at[heads * (1 - core) + h], kvb.at[h, :, rows, :], kv_send.at[h, 0], kv_recv.at[h, 0], sibling)

    def x_local(n, h):
        src, dst = ((q_in, qv), (do_in, dov))[n]
        return pltpu.make_async_copy(
            src.at[pl.ds(qheads * core + group * h, group)], dst.at[core, pl.ds(group * h, group)], x_loc.at[n, h]
        )

    def x_swap(n, h, half=core):
        src, dst = ((q_in, qv), (do_in, dov))[n]
        return remote(
            src.at[pl.ds(qheads * (1 - core) + group * h, group)],
            dst.at[half, pl.ds(group * h, group)],
            x_send.at[n, h],
            x_recv.at[n, h],
            sibling,
        )

    def to_up(h):
        return remote(part(h, 1024), part(h, 0), kv_send.at[h, 4], kv_recv.at[h, 4], up)

    def to_right(h):
        return remote(part(h, pos_right), part(h, 768), kv_send.at[h, 1], kv_recv.at[h, 1], right)

    def to_left(h):
        return remote(part(h, pos_left), part(h, 256), kv_send.at[h, 3], kv_recv.at[h, 3], left)

    def to_onward(h):
        return remote(part(h, pos_mid), part(h, 512), kv_send.at[h, 2], kv_recv.at[h, 2], onward)

    def own_ready(h):
        kv_local(h).wait()
        kv_swap(h, other_rows).wait_recv()
        to_up(h).start()

        @pl.when(x < chips - 1)
        def _():
            to_right(h).start()

        @pl.when(x == 0)
        def _():
            to_left(h).start()

    def far_ready(h):
        to_up(h).wait_recv()

        @pl.when(x == chips - 1)
        def _():
            to_right(h).start()

        @pl.when(x > 0)
        def _():
            to_left(h).start()

    def relay(h):
        @pl.when(core == 0)
        def _():
            to_right(h).wait_recv()

        @pl.when(core == 1)
        def _():
            to_left(h).wait_recv()

        to_onward(h).start()

    def all_ready(h):
        @pl.when(core == 1)
        def _():
            to_right(h).wait_recv()

        @pl.when(core == 0)
        def _():
            to_left(h).wait_recv()

        to_onward(h).wait_recv()
        for n in range(2):
            x_local(n, h).wait()
            x_swap(n, h, 1 - core).wait_recv()

    def back(h, n, device):
        return remote(sbuf.at[h, n], rbuf.at[h, n], g_send.at[h, n], g_recv.at[h, n], device)

    def send_back(h, n, pos, device):
        rows = pl.ds(pos, CHIP)
        sbuf[h, n] = acc[h, :, rows, :].astype(jnp.bfloat16)
        back(h, n, device).start()

    def add_back(h, n, device, pos):
        back(h, n, device).wait_recv()
        rows = pl.ds(pl.multiple_of(pos, 256), CHIP)
        acc[h, :, rows, :] = acc[h, :, rows, :] + rbuf[h, n].astype(jnp.float32)

    def finish_head(h):
        send_back(h, 0, 512, backward)

        @pl.when(core == 0)
        def _():
            send_back(h, 2, 256, right)

        @pl.when(core == 1)
        def _():
            send_back(h, 1, 768, left)

    def second_back(h):
        add_back(h, 0, backward, pos_mid)

        @pl.when(core == 0)
        def _():
            send_back(h, 1, 768, left)

        @pl.when(core == 1)
        def _():
            send_back(h, 2, 256, right)

    def third_back(h):
        add_back(h, 1, left, pos_right)
        add_back(h, 2, right, pos_left)
        send_back(h, 3, 0, down)

    def fin_local(h):
        return pltpu.make_async_copy(
            fin.at[h, :, pl.ds(pl.multiple_of(TOK * core, TOK), TOK), :], dkv_out.at[heads * core + h], fin_loc.at[h]
        )

    def fin_swap(h, owner=core):
        return remote(
            fin.at[h, :, pl.ds(pl.multiple_of(TOK * (1 - core), TOK), TOK), :],
            dkv_out.at[heads * owner + h],
            fin_send.at[h],
            fin_recv.at[h],
            sibling,
        )

    def last_back(h):
        back(h, 3, down).wait_recv()
        rows = pl.ds(1024, CHIP)
        fin[h, 0] = ((acc[h, 0, rows, :] + rbuf[h, 3, 0].astype(jnp.float32)) * scale).astype(jnp.bfloat16)
        fin[h, 1] = (acc[h, 1, rows, :] + rbuf[h, 3, 1].astype(jnp.float32)).astype(jnp.bfloat16)
        fin_local(h).start()
        fin_swap(h).start()

    def dq_slice(h, pair):
        return pl.ds(group * h + PAIRS * pair, PAIRS)

    def dq_local(h, pair):
        return pltpu.make_async_copy(
            dqv.at[core, dq_slice(h, pair)],
            dq_out.at[pl.ds(qheads * core + group * h + PAIRS * pair, PAIRS)],
            dq_loc.at[h, pair],
        )

    def dq_swap(h, pair, owner=core):
        return remote(
            dqv.at[1 - core, dq_slice(h, pair)],
            dq_out.at[pl.ds(qheads * owner + group * h + PAIRS * pair, PAIRS)],
            dq_send.at[h, pair],
            dq_recv.at[h, pair],
            sibling,
        )

    for h in range(heads):
        kv_local(h).start()
        kv_swap(h).start()
    for h in range(heads):
        for n in range(2):
            x_local(n, h).start()
            x_swap(n, h).start()

    for h in range(heads):
        own_ready(h)

    start_pos = chip * CHIP
    token = lax.broadcasted_iota(jnp.int32, (8, CHIP), 1) + start_pos

    def doc(number, carry):
        begin, doc_start = carry
        return begin + lengths[number], jnp.where(token >= begin, begin, doc_start)

    _, doc_start = lax.fori_loop(0, lengths.shape[0], doc, (jnp.int32(0), jnp.zeros((8, CHIP), jnp.int32)))
    for t in range(2):
        low = doc_start[0:1, TOK * t : TOK * (t + 1)] - (start_pos + TOK * t) + 1024
        high = lax.broadcasted_iota(jnp.int32, (1, TOK), 1) + 1024
        for tile in range(SPAN // TILE):
            key = lax.broadcasted_iota(jnp.int32, (TILE, TOK), 0) + tile * TILE
            bias[t, pl.ds(tile * TILE, TILE), :] = jnp.where((key >= low) & (key <= high), 0.0, -1e30)

    far_ready(0)
    for h in range(heads):
        for n in range(2):
            for tile in range(WINDOW // CHIP):
                acc[h, n, pl.ds(tile * CHIP, CHIP), :] = jnp.zeros((CHIP, TOK), jnp.float32)
    far_ready(1)
    relay(0)
    all_ready(0)

    hooks = {
        1: [lambda: relay(1), lambda: far_ready(2)],
        2: [lambda: relay(2), lambda: far_ready(3)],
        3: [lambda: relay(3)],
        4: [lambda: finish_head(0), lambda: all_ready(1)],
        7: [lambda: second_back(0)],
        8: [lambda: finish_head(1), lambda: all_ready(2)],
        10: [lambda: third_back(0)],
        11: [lambda: second_back(1)],
        12: [lambda: finish_head(2), lambda: all_ready(3)],
        13: [lambda: last_back(0)],
        14: [lambda: third_back(1)],
        15: [lambda: second_back(2)],
    }
    pairs = group // PAIRS
    steps = heads * 2 * pairs

    for step in range(steps):
        for each in hooks.get(step, ()):
            each()
        h = step // (2 * pairs)
        t = step // pairs % 2
        pair = step % pairs
        off = t * TOK
        q = qv[t, dq_slice(h, pair)].reshape(ROWS, TOK)
        do = dov[t, dq_slice(h, pair)].reshape(ROWS, TOK)
        tiles = [pl.ds(tile * TILE, TILE) for tile in range(SPAN // TILE)]
        keys = [pl.ds(off + tile * TILE, TILE) for tile in range(SPAN // TILE)]
        top = jnp.full((8, ROWS), -jnp.inf, jnp.float32)
        for tile, key in zip(tiles, keys):
            score = lax.dot_general(kvb[h, 0, key, :], q, NT, preferred_element_type=jnp.float32)
            score = score + jnp.concatenate([bias[t, tile, :]] * PAIRS, axis=1)
            s_scr[tile, :] = score
            dp_scr[tile, :] = lax.dot_general(kvb[h, 1, key, :], do, NT, preferred_element_type=jnp.float32)
            top = jnp.maximum(top, jnp.max(score.reshape(TILE // 8, 8, ROWS), axis=0))
        factor = scale * LOG2E
        shift = jnp.max(top, axis=0, keepdims=True) * factor
        weight = jnp.zeros((8, ROWS), jnp.float32)
        weighted = jnp.zeros((8, ROWS), jnp.float32)
        for tile in tiles:
            expo = jnp.exp2(s_scr[tile, :] * factor - shift)
            s_scr[tile, :] = expo
            weight = weight + jnp.sum(expo.reshape(TILE // 8, 8, ROWS), axis=0)
            weighted = weighted + jnp.sum((expo * dp_scr[tile, :]).reshape(TILE // 8, 8, ROWS), axis=0)
        inverse = 1.0 / jnp.sum(weight, axis=0, keepdims=True)
        delta = jnp.sum(weighted, axis=0, keepdims=True) * inverse
        for tile, key in zip(tiles, keys):
            prob = s_scr[tile, :] * inverse
            dscore = (prob * (dp_scr[tile, :] - delta)).astype(jnp.bfloat16)
            dsb[tile, :] = dscore
            acc[h, 1, key, :] += jnp.dot(prob.astype(jnp.bfloat16), do, preferred_element_type=jnp.float32)
            acc[h, 0, key, :] += jnp.dot(dscore, q, preferred_element_type=jnp.float32)
        dq = lax.dot_general(dsb[...], kvb[h, 0, pl.ds(off, SPAN), :], TN, preferred_element_type=jnp.float32)
        dqv[t, dq_slice(h, pair)] = (dq * scale).astype(jnp.bfloat16).reshape(PAIRS, TOK, TOK)

        @pl.when(core == t)
        def _(h=h, pair=pair):
            dq_local(h, pair).start()

        @pl.when(core == 1 - t)
        def _(h=h, pair=pair):
            dq_swap(h, pair).start()

    finish_head(3)
    last_back(1)
    third_back(2)
    second_back(3)
    last_back(2)
    third_back(3)
    last_back(3)

    for h in range(heads):
        kv_swap(h).wait_send()
        to_up(h).wait_send()
        to_right(h).wait_send()
        to_left(h).wait_send()
        to_onward(h).wait_send()
        for n in range(2):
            x_swap(n, h).wait_send()
        for n, device in enumerate((backward, left, right, down)):
            back(h, n, device).wait_send()
        for pair in range(pairs):
            dq_local(h, pair).wait()
            dq_swap(h, pair).wait_send()
            dq_swap(h, pair, 1 - core).wait_recv()
        fin_local(h).wait()
        fin_swap(h).wait_send()
        fin_swap(h, 1 - core).wait_recv()


def solution(mesh):
    blocks, chips = mesh.shape["ctx"], mesh.shape["uly"] // 2

    def local(queries, keys, values, grad_out, doc_lengths):
        tokens, query_heads, dim = queries.shape
        kv_heads = keys.shape[1]
        heads, group = kv_heads // 2, query_heads // kv_heads
        qheads = heads * group
        pairs = group // PAIRS
        q = jnp.transpose(queries, (1, 0, 2))
        do = jnp.transpose(grad_out, (1, 0, 2))
        kv = jnp.stack([jnp.transpose(keys, (1, 0, 2)), jnp.transpose(values, (1, 0, 2))], axis=1)
        bf16, f32 = jnp.bfloat16, jnp.float32
        vmem, dma = pltpu.VMEM, pltpu.SemaphoreType.DMA
        anywhere = pl.BlockSpec(memory_space=pl.ANY)

        def body(*refs):
            kernel(heads, group, chips, blocks, *refs)

        dq, dkv = pl.pallas_call(
            body,
            out_shape=[
                jax.ShapeDtypeStruct((query_heads, tokens, dim), bf16),
                jax.ShapeDtypeStruct((kv_heads, 2, tokens, dim), bf16),
            ],
            in_specs=[pl.BlockSpec(memory_space=pltpu.SMEM), anywhere, anywhere, anywhere],
            out_specs=[anywhere, anywhere],
            scratch_shapes=[
                vmem((heads, 2, WINDOW, dim), bf16),
                vmem((2, qheads, tokens, dim), bf16),
                vmem((2, qheads, tokens, dim), bf16),
                vmem((2, SPAN, TOK), f32),
                vmem((SPAN, ROWS), f32),
                vmem((SPAN, ROWS), f32),
                vmem((SPAN, ROWS), bf16),
                vmem((heads, 2, WINDOW, dim), f32),
                vmem((2, qheads, tokens, dim), bf16),
                vmem((heads, 4, 2, CHIP, dim), bf16),
                vmem((heads, 4, 2, CHIP, dim), bf16),
                vmem((heads, 2, CHIP, dim), bf16),
                dma((heads,)),
                dma((heads, 5)),
                dma((heads, 5)),
                dma((2, heads)),
                dma((2, heads)),
                dma((2, heads)),
                dma((heads, 4)),
                dma((heads, 4)),
                dma((heads, pairs)),
                dma((heads, pairs)),
                dma((heads, pairs)),
                dma((heads,)),
                dma((heads,)),
                dma((heads,)),
            ],
            compiler_params=pltpu.CompilerParams(
                collective_id=0, has_side_effects=True, vmem_limit_bytes=48 << 20
            ),
        )(doc_lengths, q, do, kv)
        return (
            jnp.transpose(dq, (1, 0, 2)),
            jnp.transpose(dkv[:, 0], (1, 0, 2)),
            jnp.transpose(dkv[:, 1], (1, 0, 2)),
        )

    spread = P(("ctx", "uly"), None, None)
    return jax.shard_map(
        local,
        mesh=mesh,
        in_specs=(spread, spread, spread, spread, P()),
        out_specs=(spread, spread, spread),
        check_vma=False,
    )
```

```python
import jax
import jax.numpy as jnp
from jax import lax
from jax.experimental import pallas as pl
from jax.experimental.pallas import tpu as pltpu
from jax.sharding import PartitionSpec as P

MESH = pl.DeviceIdType.MESH
NT = (((1,), (1,)), ((), ()))
TN = (((0,), (0,)), ((), ()))
LOG2E = 1.4426950408889634

TOK = 128
CHIP = 256
WINDOW = 1280
SPAN = 1152
TILE = 128
ROWS = 256
PAIRS = ROWS // TOK


def kernel(
    heads,
    group,
    chips,
    blocks,
    lengths,
    q_in,
    do_in,
    kv_in,
    dq_out,
    dkv_out,
    kvb,
    qv,
    dov,
    bias,
    s_scr,
    dp_scr,
    dsb,
    acc,
    dqv,
    sbuf,
    rbuf,
    fin,
    swap_send,
    swap_recv,
    kv_send,
    kv_recv,
    x_send,
    x_recv,
    g_send,
    g_recv,
    dq_send,
    dq_recv,
    fin_send,
    fin_recv,
):
    ctx = lax.axis_index("ctx")
    uly = lax.axis_index("uly")
    x, core = uly // 2, uly % 2
    qheads = heads * group
    scale = TOK**-0.5
    chip = ctx * chips + x
    total = blocks * chips
    pairs = group // PAIRS
    steps = heads * 2 * pairs

    def at(block, place, its_core):
        return (block % blocks, (place % chips) * 2 + its_core)

    def device(number):
        number = (number + total) % total
        return (number // chips, (number % chips) * 2 + core)

    sibling = (ctx, uly + 1 - 2 * core)

    def up(its_core=core):
        return at(ctx + 1, x, its_core)

    def down(its_core=core):
        return at(ctx + blocks - 1, x, its_core)

    def right(its_core=core):
        return at(ctx, x + 1, its_core)

    def left(its_core=core):
        return at(ctx, x + chips - 1, its_core)

    onward = device(chip + 1 - 2 * core)
    backward = device(chip - 1 + 2 * core)

    pos_right = 1024 * (1 - x // (chips - 1))
    pos_left = 1024 * (1 - (x + chips - 2) // (chips - 1))
    pos_mid = 768 - 512 * core

    barrier = pltpu.get_barrier_semaphore()
    partners = [sibling, onward, backward]
    for its_core in (0, 1):
        partners += [up(its_core), down(its_core), right(its_core), left(its_core)]
    for each in partners:
        pl.semaphore_signal(barrier, inc=1, device_id=each, device_id_type=MESH)
    pl.semaphore_wait(barrier, len(partners))

    def remote(src, dst, send, recv, target):
        return pltpu.make_async_remote_copy(
            src_ref=src, dst_ref=dst, send_sem=send, recv_sem=recv, device_id=target, device_id_type=MESH
        )

    def rows_at(pos, half):
        start = pos + TOK * half
        return pl.ds(start if isinstance(start, int) else pl.multiple_of(start, TOK), TOK)

    def swap(h, half=core):
        return remote(
            kv_in.at[heads * (1 - core) + h],
            kvb.at[h, :, rows_at(1024, half), :],
            swap_send.at[h],
            swap_recv.at[h],
            sibling,
        )

    def x_swap(n, h, half=core):
        src, dst = ((q_in, qv), (do_in, dov))[n]
        return remote(
            src.at[pl.ds(qheads * (1 - core) + group * h, group)],
            dst.at[half, pl.ds(group * h, group)],
            x_send.at[n, h],
            x_recv.at[n, h],
            sibling,
        )

    def send_own(h, slot, target):
        for j in (0, 1):
            remote(
                kv_in.at[heads * j + h],
                kvb.at[h, :, rows_at(1024 - 256 * slot, core), :],
                kv_send.at[h, slot - 1, j],
                kv_recv.at[h, slot - 1, core],
                target(j),
            ).start()

    def forward(h, slot, pos, half, target):
        return remote(
            kvb.at[h, :, rows_at(pos, half), :],
            kvb.at[h, :, rows_at(1024 - 256 * slot, half), :],
            kv_send.at[h, slot - 1, half],
            kv_recv.at[h, slot - 1, half],
            target,
        )

    def own_send(h):
        send_own(h, 4, up)

        @pl.when(x < chips - 1)
        def _():
            send_own(h, 1, right)

        @pl.when(x == 0)
        def _():
            send_own(h, 3, left)

    def far_ready(h):
        for half in (0, 1):
            forward(h, 4, 1024, half, up()).wait_recv()

            @pl.when(x == chips - 1)
            def _():
                forward(h, 1, 0, half, right()).start()

            @pl.when(x > 0)
            def _():
                forward(h, 3, 0, half, left()).start()

    def relay(h):
        for half in (0, 1):

            @pl.when(core == 0)
            def _():
                forward(h, 1, 0, half, right()).wait_recv()

            @pl.when(core == 1)
            def _():
                forward(h, 3, 0, half, left()).wait_recv()

            forward(h, 2, pos_mid, half, onward).start()

    def all_ready(h):
        for half in (0, 1):

            @pl.when(core == 1)
            def _():
                forward(h, 1, 0, half, right()).wait_recv()

            @pl.when(core == 0)
            def _():
                forward(h, 3, 0, half, left()).wait_recv()

            forward(h, 2, 0, half, onward).wait_recv()
        swap(h, 1 - core).wait_recv()
        for n in range(2):
            x_swap(n, h, 1 - core).wait_recv()

    def back(h, n, i, target):
        return remote(sbuf.at[h, n, i], rbuf.at[h, n, i], g_send.at[h, n, i], g_recv.at[h, n, i], target)

    def send_back(h, n, i, pos, target):
        sbuf[h, n, i] = acc[h, i, pl.ds(pos, CHIP), :].astype(jnp.bfloat16)
        back(h, n, i, target).start()

    def add_back(h, n, i, target, pos):
        back(h, n, i, target).wait_recv()
        rows = pl.ds(pl.multiple_of(pos, 256), CHIP)
        acc[h, i, rows, :] = acc[h, i, rows, :] + rbuf[h, n, i].astype(jnp.float32)

    def finish_head(h):
        for i in range(2):
            send_back(h, 0, i, 512, backward)

            @pl.when(core == 0)
            def _():
                send_back(h, 2, i, 256, right())

            @pl.when(core == 1)
            def _():
                send_back(h, 1, i, 768, left())

    def second_back(h):
        for i in range(2):
            add_back(h, 0, i, backward, pos_mid)

            @pl.when(core == 0)
            def _():
                send_back(h, 1, i, 768, left())

            @pl.when(core == 1)
            def _():
                send_back(h, 2, i, 256, right())

    def third_back(h):
        for i in range(2):
            add_back(h, 1, i, left(), pos_right)
            add_back(h, 2, i, right(), pos_left)
            send_back(h, 3, i, 0, down())

    def fin_swap(h, i, owner=core):
        return remote(fin.at[h, i], dkv_out.at[heads * owner + h, i], fin_send.at[h, i], fin_recv.at[h, i], sibling)

    def last_back(h):
        for i in range(2):
            back(h, 3, i, down()).wait_recv()
            whole = acc[h, i, pl.ds(1024, CHIP), :] + rbuf[h, 3, i].astype(jnp.float32)
            if i == 0:
                whole = whole * scale
            whole = whole.astype(jnp.bfloat16)
            for k in (0, 1):

                @pl.when(core == k)
                def _():
                    dkv_out[heads * k + h, i] = whole[TOK * k : TOK * (k + 1)]
                    fin[h, i] = whole[TOK * (1 - k) : TOK * (2 - k)]

            fin_swap(h, i).start()

    def dq_swap(h, pair, owner=core):
        return remote(
            dqv.at[pl.ds(group * h + PAIRS * pair, PAIRS)],
            dq_out.at[pl.ds(qheads * owner + group * h + PAIRS * pair, PAIRS)],
            dq_send.at[h, pair],
            dq_recv.at[h, pair],
            sibling,
        )

    for h in range(heads):
        own_send(h)
        swap(h).start()
        for n in range(2):
            x_swap(n, h).start()
    for k in (0, 1):

        @pl.when(core == k)
        def _():
            for h in range(heads):
                kvb[h, :, pl.ds(1024 + TOK * k, TOK), :] = kv_in[heads * k + h]
            for head in range(qheads):
                qv[k, head] = q_in[qheads * k + head]
                dov[k, head] = do_in[qheads * k + head]

    start_pos = chip * CHIP
    token = lax.broadcasted_iota(jnp.int32, (8, CHIP), 1) + start_pos

    def doc(number, carry):
        begin, doc_start = carry
        return begin + lengths[number], jnp.where(token >= begin, begin, doc_start)

    _, doc_start = lax.fori_loop(0, lengths.shape[0], doc, (jnp.int32(0), jnp.zeros((8, CHIP), jnp.int32)))
    for t in range(2):
        low = doc_start[0:1, TOK * t : TOK * (t + 1)] - (start_pos + TOK * t) + 1024
        high = lax.broadcasted_iota(jnp.int32, (1, TOK), 1) + 1024
        for tile in range(SPAN // TILE):
            key = lax.broadcasted_iota(jnp.int32, (TILE, TOK), 0) + tile * TILE
            bias[t, pl.ds(tile * TILE, TILE), :] = jnp.where((key >= low) & (key <= high), 0.0, -1e30)

    far_ready(0)
    for h in range(heads):
        for n in range(2):
            for tile in range(WINDOW // CHIP):
                acc[h, n, pl.ds(tile * CHIP, CHIP), :] = jnp.zeros((CHIP, TOK), jnp.float32)
    far_ready(1)
    relay(0)
    all_ready(0)

    hooks = {
        1: [lambda: relay(1), lambda: far_ready(2)],
        2: [lambda: relay(2), lambda: far_ready(3)],
        3: [lambda: relay(3)],
        4: [lambda: finish_head(0), lambda: all_ready(1)],
        7: [lambda: second_back(0)],
        8: [lambda: finish_head(1), lambda: all_ready(2)],
        10: [lambda: third_back(0)],
        11: [lambda: second_back(1)],
        12: [lambda: finish_head(2), lambda: all_ready(3)],
        13: [lambda: last_back(0)],
        14: [lambda: third_back(1)],
        15: [lambda: second_back(2)],
    }

    for step in range(steps):
        for each in hooks.get(step, ()):
            each()
        h = step // (2 * pairs)
        t = step // pairs % 2
        pair = step % pairs
        off = t * TOK
        mine = pl.ds(group * h + PAIRS * pair, PAIRS)
        q = qv[t, mine].reshape(ROWS, TOK)
        do = dov[t, mine].reshape(ROWS, TOK)
        tiles = [pl.ds(tile * TILE, TILE) for tile in range(SPAN // TILE)]
        keys = [pl.ds(off + tile * TILE, TILE) for tile in range(SPAN // TILE)]
        top = jnp.full((8, ROWS), -jnp.inf, jnp.float32)
        for tile, key in zip(tiles, keys):
            score = lax.dot_general(kvb[h, 0, key, :], q, NT, preferred_element_type=jnp.float32)
            score = score + jnp.concatenate([bias[t, tile, :]] * PAIRS, axis=1)
            s_scr[tile, :] = score
            dp_scr[tile, :] = lax.dot_general(kvb[h, 1, key, :], do, NT, preferred_element_type=jnp.float32)
            top = jnp.maximum(top, jnp.max(score.reshape(TILE // 8, 8, ROWS), axis=0))
        factor = scale * LOG2E
        shift = jnp.max(top, axis=0, keepdims=True) * factor
        weight = jnp.zeros((8, ROWS), jnp.float32)
        weighted = jnp.zeros((8, ROWS), jnp.float32)
        for tile in tiles:
            expo = jnp.exp2(s_scr[tile, :] * factor - shift)
            s_scr[tile, :] = expo
            weight = weight + jnp.sum(expo.reshape(TILE // 8, 8, ROWS), axis=0)
            weighted = weighted + jnp.sum((expo * dp_scr[tile, :]).reshape(TILE // 8, 8, ROWS), axis=0)
        inverse = 1.0 / jnp.sum(weight, axis=0, keepdims=True)
        delta = jnp.sum(weighted, axis=0, keepdims=True) * inverse
        for tile, key in zip(tiles, keys):
            prob = s_scr[tile, :] * inverse
            dscore = (prob * (dp_scr[tile, :] - delta)).astype(jnp.bfloat16)
            dsb[tile, :] = dscore
            acc[h, 1, key, :] += jnp.dot(prob.astype(jnp.bfloat16), do, preferred_element_type=jnp.float32)
            acc[h, 0, key, :] += jnp.dot(dscore, q, preferred_element_type=jnp.float32)
        dq = lax.dot_general(dsb[...], kvb[h, 0, pl.ds(off, SPAN), :], TN, preferred_element_type=jnp.float32)
        dq = (dq * scale).astype(jnp.bfloat16).reshape(PAIRS, TOK, TOK)

        @pl.when(core == t)
        def _():
            dq_out[pl.ds(qheads * t + group * h + PAIRS * pair, PAIRS)] = dq

        @pl.when(core == 1 - t)
        def _():
            dqv[mine] = dq
            dq_swap(h, pair).start()

    finish_head(3)
    last_back(1)
    third_back(2)
    second_back(3)
    last_back(2)
    third_back(3)
    last_back(3)

    for h in range(heads):
        swap(h).wait_send()
        for slot, target in ((1, right()), (2, onward), (3, left()), (4, up())):
            for half in (0, 1):
                forward(h, slot, 0, half, target).wait_send()
        for n in range(2):
            x_swap(n, h).wait_send()
        for i in range(2):
            for n, target in enumerate((backward, left(), right(), down())):
                back(h, n, i, target).wait_send()
            fin_swap(h, i).wait_send()
            fin_swap(h, i, 1 - core).wait_recv()
        for pair in range(pairs):
            dq_swap(h, pair).wait_send()
            dq_swap(h, pair, 1 - core).wait_recv()


def solution(mesh):
    blocks, chips = mesh.shape["ctx"], mesh.shape["uly"] // 2

    def local(queries, keys, values, grad_out, doc_lengths):
        tokens, query_heads, dim = queries.shape
        kv_heads = keys.shape[1]
        heads, group = kv_heads // 2, query_heads // kv_heads
        qheads = heads * group
        pairs = group // PAIRS
        q = jnp.transpose(queries, (1, 0, 2))
        do = jnp.transpose(grad_out, (1, 0, 2))
        kv = jnp.stack([jnp.transpose(keys, (1, 0, 2)), jnp.transpose(values, (1, 0, 2))], axis=1)
        bf16, f32 = jnp.bfloat16, jnp.float32
        vmem, dma = pltpu.VMEM, pltpu.SemaphoreType.DMA
        inside = pl.BlockSpec(memory_space=pltpu.VMEM)

        def body(*refs):
            kernel(heads, group, chips, blocks, *refs)

        dq, dkv = pl.pallas_call(
            body,
            out_shape=[
                jax.ShapeDtypeStruct((query_heads, tokens, dim), bf16),
                jax.ShapeDtypeStruct((kv_heads, 2, tokens, dim), bf16),
            ],
            in_specs=[pl.BlockSpec(memory_space=pltpu.SMEM), inside, inside, inside],
            out_specs=[inside, inside],
            scratch_shapes=[
                vmem((heads, 2, WINDOW, dim), bf16),
                vmem((2, qheads, tokens, dim), bf16),
                vmem((2, qheads, tokens, dim), bf16),
                vmem((2, SPAN, TOK), f32),
                vmem((SPAN, ROWS), f32),
                vmem((SPAN, ROWS), f32),
                vmem((SPAN, ROWS), bf16),
                vmem((heads, 2, WINDOW, dim), f32),
                vmem((qheads, tokens, dim), bf16),
                vmem((heads, 4, 2, CHIP, dim), bf16),
                vmem((heads, 4, 2, CHIP, dim), bf16),
                vmem((heads, 2, TOK, dim), bf16),
                dma((heads,)),
                dma((heads,)),
                dma((heads, 4, 2)),
                dma((heads, 4, 2)),
                dma((2, heads)),
                dma((2, heads)),
                dma((heads, 4, 2)),
                dma((heads, 4, 2)),
                dma((heads, pairs)),
                dma((heads, pairs)),
                dma((heads, 2)),
                dma((heads, 2)),
            ],
            compiler_params=pltpu.CompilerParams(
                collective_id=0, has_side_effects=True, vmem_limit_bytes=48 << 20
            ),
        )(doc_lengths, q, do, kv)
        return (
            jnp.transpose(dq, (1, 0, 2)),
            jnp.transpose(dkv[:, 0], (1, 0, 2)),
            jnp.transpose(dkv[:, 1], (1, 0, 2)),
        )

    spread = P(("ctx", "uly"), None, None)
    return jax.shard_map(
        local,
        mesh=mesh,
        in_specs=(spread, spread, spread, spread, P()),
        out_specs=(spread, spread, spread),
        check_vma=False,
    )
```

```python
import jax
import jax.numpy as jnp
from jax import lax
from jax.experimental import pallas as pl
from jax.experimental.pallas import tpu as pltpu
from jax.sharding import PartitionSpec as P

MESH = pl.DeviceIdType.MESH
NT = (((1,), (1,)), ((), ()))
TN = (((0,), (0,)), ((), ()))
LOG2E = 1.4426950408889634

TOK = 128
CHIP = 256
WINDOW = 1280
SPAN = 1152
TILE = 128
ROWS = 256
PAIRS = ROWS // TOK


def kernel(
    heads,
    group,
    chips,
    blocks,
    lengths_in,
    q_in,
    do_in,
    k_in,
    v_in,
    dq_out,
    dk_out,
    dv_out,
    lengths,
    q_raw,
    do_raw,
    kv_raw,
    kv_own,
    q_swap,
    do_swap,
    dqh,
    dkvh,
    kvb,
    qv,
    dov,
    bias,
    s_scr,
    dp_scr,
    dsb,
    acc,
    dqv,
    sbuf,
    rbuf,
    fin,
    swap_send,
    swap_recv,
    kv_send,
    kv_recv,
    x_send,
    x_recv,
    g_send,
    g_recv,
    dq_send,
    dq_recv,
    fin_send,
    fin_recv,
    in_sem,
):
    ctx = lax.axis_index("ctx")
    uly = lax.axis_index("uly")
    x, core = uly // 2, uly % 2
    qheads = heads * group
    scale = TOK**-0.5
    chip = ctx * chips + x
    total = blocks * chips
    pairs = group // PAIRS
    steps = heads * 2 * pairs

    def at(block, place, its_core):
        return (block % blocks, (place % chips) * 2 + its_core)

    def device(number):
        number = (number + total) % total
        return (number // chips, (number % chips) * 2 + core)

    sibling = (ctx, uly + 1 - 2 * core)

    def up(its_core=core):
        return at(ctx + 1, x, its_core)

    def down(its_core=core):
        return at(ctx + blocks - 1, x, its_core)

    def right(its_core=core):
        return at(ctx, x + 1, its_core)

    def left(its_core=core):
        return at(ctx, x + chips - 1, its_core)

    onward = device(chip + 1 - 2 * core)
    backward = device(chip - 1 + 2 * core)

    pos_right = 1024 * (1 - x // (chips - 1))
    pos_left = 1024 * (1 - (x + chips - 2) // (chips - 1))
    pos_mid = 768 - 512 * core

    sources = (k_in, v_in, q_in, do_in, lengths_in)
    places = (kv_raw.at[0], kv_raw.at[1], q_raw, do_raw, lengths)
    loads = [pltpu.make_async_copy(src, dst, in_sem.at[n]) for n, (src, dst) in enumerate(zip(sources, places))]
    for load in loads:
        load.start()
    for n in range(2):
        loads[n].wait()
        kv_own[n] = jnp.transpose(kv_raw[n], (1, 0, 2))

    barrier = pltpu.get_barrier_semaphore()
    partners = [sibling, onward, backward]
    for its_core in (0, 1):
        partners += [up(its_core), down(its_core), right(its_core), left(its_core)]
    for each in partners:
        pl.semaphore_signal(barrier, inc=1, device_id=each, device_id_type=MESH)
    pl.semaphore_wait(barrier, len(partners))

    def remote(src, dst, send, recv, target):
        return pltpu.make_async_remote_copy(
            src_ref=src, dst_ref=dst, send_sem=send, recv_sem=recv, device_id=target, device_id_type=MESH
        )

    def rows_at(pos, half):
        start = pos + TOK * half
        return pl.ds(start if isinstance(start, int) else pl.multiple_of(start, TOK), TOK)

    def swap(h, half=core):
        return remote(
            kv_own.at[:, heads * (1 - core) + h],
            kvb.at[h, :, rows_at(1024, half), :],
            swap_send.at[h],
            swap_recv.at[h],
            sibling,
        )

    def x_swap(n, h, half=core):
        src, dst = ((q_swap, qv), (do_swap, dov))[n]
        return remote(
            src.at[pl.ds(group * h, group)],
            dst.at[half, pl.ds(group * h, group)],
            x_send.at[n, h],
            x_recv.at[n, h],
            sibling,
        )

    def send_own(h, slot, target):
        for j in (0, 1):
            remote(
                kv_own.at[:, heads * j + h],
                kvb.at[h, :, rows_at(1024 - 256 * slot, core), :],
                kv_send.at[h, slot - 1, j],
                kv_recv.at[h, slot - 1, core],
                target(j),
            ).start()

    def forward(h, slot, pos, half, target):
        return remote(
            kvb.at[h, :, rows_at(pos, half), :],
            kvb.at[h, :, rows_at(1024 - 256 * slot, half), :],
            kv_send.at[h, slot - 1, half],
            kv_recv.at[h, slot - 1, half],
            target,
        )

    def own_send(h):
        @pl.when(x < chips - 1)
        def _():
            send_own(h, 1, right)

        @pl.when(x == 0)
        def _():
            send_own(h, 3, left)

    def far_ready(h):
        for half in (0, 1):
            forward(h, 4, 1024, half, up()).wait_recv()

            @pl.when(x == chips - 1)
            def _():
                forward(h, 1, 0, half, right()).start()

            @pl.when(x > 0)
            def _():
                forward(h, 3, 0, half, left()).start()

    def relay(h):
        for half in (0, 1):

            @pl.when(core == 0)
            def _():
                forward(h, 1, 0, half, right()).wait_recv()

            @pl.when(core == 1)
            def _():
                forward(h, 3, 0, half, left()).wait_recv()

            forward(h, 2, pos_mid, half, onward).start()

    def all_ready(h):
        for half in (0, 1):

            @pl.when(core == 1)
            def _():
                forward(h, 1, 0, half, right()).wait_recv()

            @pl.when(core == 0)
            def _():
                forward(h, 3, 0, half, left()).wait_recv()

            forward(h, 2, 0, half, onward).wait_recv()
        swap(h, 1 - core).wait_recv()
        for n in range(2):
            x_swap(n, h, 1 - core).wait_recv()

    def back(h, n, i, target):
        return remote(sbuf.at[h, n, i], rbuf.at[h, n, i], g_send.at[h, n, i], g_recv.at[h, n, i], target)

    def send_back(h, n, i, pos, target):
        sbuf[h, n, i] = acc[h, i, pl.ds(pos, CHIP), :].astype(jnp.bfloat16)
        back(h, n, i, target).start()

    def add_back(h, n, i, target, pos):
        back(h, n, i, target).wait_recv()
        rows = pl.ds(pl.multiple_of(pos, 256), CHIP)
        acc[h, i, rows, :] = acc[h, i, rows, :] + rbuf[h, n, i].astype(jnp.float32)

    def finish_head(h):
        for i in range(2):
            send_back(h, 0, i, 512, backward)

            @pl.when(core == 0)
            def _():
                send_back(h, 2, i, 256, right())

            @pl.when(core == 1)
            def _():
                send_back(h, 1, i, 768, left())

    def second_back(h):
        for i in range(2):
            add_back(h, 0, i, backward, pos_mid)

            @pl.when(core == 0)
            def _():
                send_back(h, 1, i, 768, left())

            @pl.when(core == 1)
            def _():
                send_back(h, 2, i, 256, right())

    def third_back(h):
        for i in range(2):
            add_back(h, 1, i, left(), pos_right)
            add_back(h, 2, i, right(), pos_left)
            send_back(h, 3, i, 0, down())

    def fin_swap(h, i, owner=core):
        return remote(fin.at[h, i], dkvh.at[i, heads * owner + h], fin_send.at[h, i], fin_recv.at[h, i], sibling)

    def last_back(h):
        for i in range(2):
            back(h, 3, i, down()).wait_recv()
            whole = acc[h, i, pl.ds(1024, CHIP), :] + rbuf[h, 3, i].astype(jnp.float32)
            if i == 0:
                whole = whole * scale
            whole = whole.astype(jnp.bfloat16)
            for k in (0, 1):

                @pl.when(core == k)
                def _():
                    dkvh[i, heads * k + h] = whole[TOK * k : TOK * (k + 1)]
                    fin[h, i] = whole[TOK * (1 - k) : TOK * (2 - k)]

            fin_swap(h, i).start()

    def dq_swap(h, pair, owner=core):
        return remote(
            dqv.at[pl.ds(group * h + PAIRS * pair, PAIRS)],
            dqh.at[pl.ds(qheads * owner + group * h + PAIRS * pair, PAIRS)],
            dq_send.at[h, pair],
            dq_recv.at[h, pair],
            sibling,
        )

    for h in range(heads):
        send_own(h, 4, up)
        if h < 2:
            own_send(h)
        swap(h).start()
    loads[2].wait()
    loads[3].wait()
    for k in (0, 1):

        @pl.when(core == k)
        def _():
            other = pl.ds(qheads * (1 - k), qheads)
            q_swap[...] = jnp.transpose(q_raw[:, other, :], (1, 0, 2))
            do_swap[...] = jnp.transpose(do_raw[:, other, :], (1, 0, 2))

    for h in range(heads):
        for n in range(2):
            x_swap(n, h).start()
    far_ready(0)
    for k in (0, 1):

        @pl.when(core == k)
        def _():
            mine = pl.ds(qheads * k, qheads)
            qv[k] = jnp.transpose(q_raw[:, mine, :], (1, 0, 2))
            dov[k] = jnp.transpose(do_raw[:, mine, :], (1, 0, 2))
            for h in range(heads):
                kvb[h, :, pl.ds(1024 + TOK * k, TOK), :] = kv_own[:, heads * k + h]

    loads[4].wait()
    start_pos = chip * CHIP
    token = lax.broadcasted_iota(jnp.int32, (8, CHIP), 1) + start_pos

    def doc(number, carry):
        begin, doc_start = carry
        return begin + lengths[number], jnp.where(token >= begin, begin, doc_start)

    _, doc_start = lax.fori_loop(0, lengths.shape[0], doc, (jnp.int32(0), jnp.zeros((8, CHIP), jnp.int32)))
    for t in range(2):
        low = doc_start[0:1, TOK * t : TOK * (t + 1)] - (start_pos + TOK * t) + 1024
        high = lax.broadcasted_iota(jnp.int32, (1, TOK), 1) + 1024
        for tile in range(SPAN // TILE):
            key = lax.broadcasted_iota(jnp.int32, (TILE, TOK), 0) + tile * TILE
            bias[t, pl.ds(tile * TILE, TILE), :] = jnp.where((key >= low) & (key <= high), 0.0, -1e30)

    for h in range(heads):
        for n in range(2):
            for tile in range(WINDOW // CHIP):
                acc[h, n, pl.ds(tile * CHIP, CHIP), :] = jnp.zeros((CHIP, TOK), jnp.float32)
    relay(0)
    own_send(2)
    far_ready(1)
    all_ready(0)

    hooks = {
        1: [lambda: relay(1), lambda: own_send(3), lambda: far_ready(2)],
        2: [lambda: far_ready(3)],
        3: [lambda: relay(2)],
        4: [lambda: finish_head(0), lambda: all_ready(1)],
        5: [lambda: relay(3)],
        7: [lambda: second_back(0)],
        8: [lambda: finish_head(1), lambda: all_ready(2)],
        10: [lambda: third_back(0)],
        11: [lambda: second_back(1)],
        12: [lambda: finish_head(2), lambda: all_ready(3)],
        13: [lambda: last_back(0)],
        14: [lambda: third_back(1)],
        15: [lambda: second_back(2)],
    }

    for step in range(steps):
        for each in hooks.get(step, ()):
            each()
        h = step // (2 * pairs)
        t = step // pairs % 2
        pair = step % pairs
        off = t * TOK
        mine = pl.ds(group * h + PAIRS * pair, PAIRS)
        q = qv[t, mine].reshape(ROWS, TOK)
        do = dov[t, mine].reshape(ROWS, TOK)
        tiles = [pl.ds(tile * TILE, TILE) for tile in range(SPAN // TILE)]
        keys = [pl.ds(off + tile * TILE, TILE) for tile in range(SPAN // TILE)]
        top = jnp.full((8, ROWS), -jnp.inf, jnp.float32)
        for tile, key in zip(tiles, keys):
            score = lax.dot_general(kvb[h, 0, key, :], q, NT, preferred_element_type=jnp.float32)
            score = score + jnp.concatenate([bias[t, tile, :]] * PAIRS, axis=1)
            s_scr[tile, :] = score
            dp_scr[tile, :] = lax.dot_general(kvb[h, 1, key, :], do, NT, preferred_element_type=jnp.float32)
            top = jnp.maximum(top, jnp.max(score.reshape(TILE // 8, 8, ROWS), axis=0))
        factor = scale * LOG2E
        shift = jnp.max(top, axis=0, keepdims=True) * factor
        weight = jnp.zeros((8, ROWS), jnp.float32)
        weighted = jnp.zeros((8, ROWS), jnp.float32)
        for tile in tiles:
            expo = jnp.exp2(s_scr[tile, :] * factor - shift)
            s_scr[tile, :] = expo
            weight = weight + jnp.sum(expo.reshape(TILE // 8, 8, ROWS), axis=0)
            weighted = weighted + jnp.sum((expo * dp_scr[tile, :]).reshape(TILE // 8, 8, ROWS), axis=0)
        inverse = 1.0 / jnp.sum(weight, axis=0, keepdims=True)
        delta = jnp.sum(weighted, axis=0, keepdims=True) * inverse
        for tile, key in zip(tiles, keys):
            prob = s_scr[tile, :] * inverse
            dscore = (prob * (dp_scr[tile, :] - delta)).astype(jnp.bfloat16)
            dsb[tile, :] = dscore
            acc[h, 1, key, :] += jnp.dot(prob.astype(jnp.bfloat16), do, preferred_element_type=jnp.float32)
            acc[h, 0, key, :] += jnp.dot(dscore, q, preferred_element_type=jnp.float32)
        dq = lax.dot_general(dsb[...], kvb[h, 0, pl.ds(off, SPAN), :], TN, preferred_element_type=jnp.float32)
        dq = (dq * scale).astype(jnp.bfloat16).reshape(PAIRS, TOK, TOK)

        @pl.when(core == t)
        def _():
            dqh[pl.ds(qheads * t + group * h + PAIRS * pair, PAIRS)] = dq

        @pl.when(core == 1 - t)
        def _():
            dqv[mine] = dq
            dq_swap(h, pair).start()

    finish_head(3)
    last_back(1)
    third_back(2)
    for h in range(heads):
        for pair in range(pairs):
            dq_swap(h, pair).wait_send()
            dq_swap(h, pair, 1 - core).wait_recv()
    for k in (0, 1):
        some = pl.ds(qheads * k, qheads)
        dq_out[:, some, :] = jnp.transpose(dqh[some], (1, 0, 2))
    second_back(3)
    last_back(2)
    third_back(3)
    last_back(3)

    for h in range(heads):
        swap(h).wait_send()
        for slot, target in ((1, right()), (2, onward), (3, left()), (4, up())):
            for half in (0, 1):
                forward(h, slot, 0, half, target).wait_send()
        for n in range(2):
            x_swap(n, h).wait_send()
        for i in range(2):
            for n, target in enumerate((backward, left(), right(), down())):
                back(h, n, i, target).wait_send()
            fin_swap(h, i).wait_send()
            fin_swap(h, i, 1 - core).wait_recv()
    dk_out[...] = jnp.transpose(dkvh[0], (1, 0, 2))
    dv_out[...] = jnp.transpose(dkvh[1], (1, 0, 2))


def solution(mesh):
    blocks, chips = mesh.shape["ctx"], mesh.shape["uly"] // 2

    def local(queries, keys, values, grad_out, doc_lengths):
        tokens, query_heads, dim = queries.shape
        kv_heads = keys.shape[1]
        heads, group = kv_heads // 2, query_heads // kv_heads
        qheads = heads * group
        pairs = group // PAIRS
        bf16, f32 = jnp.bfloat16, jnp.float32
        vmem, dma = pltpu.VMEM, pltpu.SemaphoreType.DMA
        inside = pl.BlockSpec(memory_space=pltpu.VMEM)
        outside = pl.BlockSpec(memory_space=pltpu.HBM)

        def body(*refs):
            kernel(heads, group, chips, blocks, *refs)

        return pl.pallas_call(
            body,
            out_shape=[jax.ShapeDtypeStruct(each.shape, bf16) for each in (queries, keys, values)],
            in_specs=[outside] * 5,
            out_specs=[inside] * 3,
            scratch_shapes=[
                pltpu.SMEM(doc_lengths.shape, jnp.int32),
                vmem(queries.shape, bf16),
                vmem(queries.shape, bf16),
                vmem((2,) + keys.shape, bf16),
                vmem((2, kv_heads, tokens, dim), bf16),
                vmem((qheads, tokens, dim), bf16),
                vmem((qheads, tokens, dim), bf16),
                vmem((query_heads, tokens, dim), bf16),
                vmem((2, kv_heads, tokens, dim), bf16),
                vmem((heads, 2, WINDOW, dim), bf16),
                vmem((2, qheads, tokens, dim), bf16),
                vmem((2, qheads, tokens, dim), bf16),
                vmem((2, SPAN, TOK), f32),
                vmem((SPAN, ROWS), f32),
                vmem((SPAN, ROWS), f32),
                vmem((SPAN, ROWS), bf16),
                vmem((heads, 2, WINDOW, dim), f32),
                vmem((qheads, tokens, dim), bf16),
                vmem((heads, 4, 2, CHIP, dim), bf16),
                vmem((heads, 4, 2, CHIP, dim), bf16),
                vmem((heads, 2, TOK, dim), bf16),
                dma((heads,)),
                dma((heads,)),
                dma((heads, 4, 2)),
                dma((heads, 4, 2)),
                dma((2, heads)),
                dma((2, heads)),
                dma((heads, 4, 2)),
                dma((heads, 4, 2)),
                dma((heads, pairs)),
                dma((heads, pairs)),
                dma((heads, 2)),
                dma((heads, 2)),
                dma((5,)),
            ],
            compiler_params=pltpu.CompilerParams(
                collective_id=0, has_side_effects=True, vmem_limit_bytes=48 << 20
            ),
        )(
            *[
                pltpu.with_memory_space_constraint(each, pltpu.HBM)
                for each in (doc_lengths, queries, grad_out, keys, values)
            ]
        )

    spread = P(("ctx", "uly"), None, None)
    return jax.shard_map(
        local,
        mesh=mesh,
        in_specs=(spread, spread, spread, spread, P()),
        out_specs=(spread, spread, spread),
        check_vma=False,
    )
```

```python
import jax
import jax.numpy as jnp
from jax import lax
from jax.experimental import pallas as pl
from jax.experimental.pallas import tpu as pltpu
from jax.sharding import PartitionSpec as P

MESH = pl.DeviceIdType.MESH
NT = (((1,), (1,)), ((), ()))
TN = (((0,), (0,)), ((), ()))
LOG2E = 1.4426950408889634

TOK = 128
CHIP = 256
WINDOW = 1280
SPAN = 1152
TILE = 128
ROWS = 256
PAIRS = ROWS // TOK


def kernel(
    heads,
    group,
    chips,
    blocks,
    lengths_in,
    q_in,
    do_in,
    k_in,
    v_in,
    dq_out,
    dk_out,
    dv_out,
    lengths,
    q_raw,
    do_raw,
    kv_raw,
    kv_own,
    q_swap,
    do_swap,
    dqh,
    dkvh,
    kvb,
    qv,
    dov,
    bias,
    s_scr,
    dp_scr,
    dsb,
    acc,
    dqv,
    sbuf,
    rbuf,
    fin,
    swap_send,
    swap_recv,
    kv_send,
    kv_recv,
    x_send,
    x_recv,
    g_send,
    g_recv,
    dq_send,
    dq_recv,
    fin_send,
    fin_recv,
    in_sem,
):
    ctx = lax.axis_index("ctx")
    uly = lax.axis_index("uly")
    x, core = uly // 2, uly % 2
    qheads = heads * group
    scale = TOK**-0.5
    chip = ctx * chips + x
    total = blocks * chips
    pairs = group // PAIRS
    steps = heads * 2 * pairs

    def at(block, place, its_core):
        return (block % blocks, (place % chips) * 2 + its_core)

    def device(number):
        number = (number + total) % total
        return (number // chips, (number % chips) * 2 + core)

    sibling = (ctx, uly + 1 - 2 * core)

    def up(its_core=core):
        return at(ctx + 1, x, its_core)

    def down(its_core=core):
        return at(ctx + blocks - 1, x, its_core)

    def right(its_core=core):
        return at(ctx, x + 1, its_core)

    def left(its_core=core):
        return at(ctx, x + chips - 1, its_core)

    onward = device(chip + 1 - 2 * core)
    backward = device(chip - 1 + 2 * core)

    pos_right = 1024 * (1 - x // (chips - 1))
    pos_left = 1024 * (1 - (x + chips - 2) // (chips - 1))
    pos_mid = 768 - 512 * core

    sources = (k_in, v_in, q_in, do_in, lengths_in)
    places = (kv_raw.at[0], kv_raw.at[1], q_raw, do_raw, lengths)
    loads = [pltpu.make_async_copy(src, dst, in_sem.at[n]) for n, (src, dst) in enumerate(zip(sources, places))]
    for load in loads:
        load.start()
    for n in range(2):
        loads[n].wait()
        kv_own[n] = jnp.transpose(kv_raw[n], (1, 0, 2))

    barrier = pltpu.get_barrier_semaphore()
    partners = [sibling, onward, backward]
    for its_core in (0, 1):
        partners += [up(its_core), down(its_core), right(its_core), left(its_core)]
    for each in partners:
        pl.semaphore_signal(barrier, inc=1, device_id=each, device_id_type=MESH)
    pl.semaphore_wait(barrier, len(partners))

    def remote(src, dst, send, recv, target):
        return pltpu.make_async_remote_copy(
            src_ref=src, dst_ref=dst, send_sem=send, recv_sem=recv, device_id=target, device_id_type=MESH
        )

    def rows_at(pos, half):
        start = pos + TOK * half
        return pl.ds(start if isinstance(start, int) else pl.multiple_of(start, TOK), TOK)

    def swap(h, half=core):
        return remote(
            kv_own.at[:, heads * (1 - core) + h],
            kvb.at[h, :, rows_at(1024, half), :],
            swap_send.at[h],
            swap_recv.at[h],
            sibling,
        )

    def x_swap(n, h, half=core):
        src, dst = ((q_swap, qv), (do_swap, dov))[n]
        return remote(
            src.at[pl.ds(group * h, group)],
            dst.at[half, pl.ds(group * h, group)],
            x_send.at[n, h],
            x_recv.at[n, h],
            sibling,
        )

    def send_own(h, slot, target):
        for j in (0, 1):
            remote(
                kv_own.at[:, heads * j + h],
                kvb.at[h, :, rows_at(1024 - 256 * slot, core), :],
                kv_send.at[h, slot - 1, j],
                kv_recv.at[h, slot - 1, core],
                target(j),
            ).start()

    def forward(h, slot, pos, half, target):
        return remote(
            kvb.at[h, :, rows_at(pos, half), :],
            kvb.at[h, :, rows_at(1024 - 256 * slot, half), :],
            kv_send.at[h, slot - 1, half],
            kv_recv.at[h, slot - 1, half],
            target,
        )

    def own_send(h):
        @pl.when(x < chips - 1)
        def _():
            send_own(h, 1, right)

        @pl.when(x == 0)
        def _():
            send_own(h, 3, left)

    def far_ready(h):
        for half in (0, 1):
            forward(h, 4, 1024, half, up()).wait_recv()

            @pl.when(x == chips - 1)
            def _():
                forward(h, 1, 0, half, right()).start()

            @pl.when(x > 0)
            def _():
                forward(h, 3, 0, half, left()).start()

    def relay(h):
        for half in (0, 1):

            @pl.when(core == 0)
            def _():
                forward(h, 1, 0, half, right()).wait_recv()

            @pl.when(core == 1)
            def _():
                forward(h, 3, 0, half, left()).wait_recv()

            forward(h, 2, pos_mid, half, onward).start()

    def all_ready(h):
        for half in (0, 1):

            @pl.when(core == 1)
            def _():
                forward(h, 1, 0, half, right()).wait_recv()

            @pl.when(core == 0)
            def _():
                forward(h, 3, 0, half, left()).wait_recv()

            forward(h, 2, 0, half, onward).wait_recv()
        swap(h, 1 - core).wait_recv()
        for n in range(2):
            x_swap(n, h, 1 - core).wait_recv()

    def back(h, n, i, target):
        return remote(sbuf.at[h, n, i], rbuf.at[h, n, i], g_send.at[h, n, i], g_recv.at[h, n, i], target)

    def send_back(h, n, i, pos, target):
        sbuf[h, n, i] = acc[h, i, pl.ds(pos, CHIP), :].astype(jnp.bfloat16)
        back(h, n, i, target).start()

    def add_back(h, n, i, target, pos):
        back(h, n, i, target).wait_recv()
        rows = pl.ds(pl.multiple_of(pos, 256), CHIP)
        acc[h, i, rows, :] = acc[h, i, rows, :] + rbuf[h, n, i].astype(jnp.float32)

    def finish_head(h):
        for i in range(2):
            send_back(h, 0, i, 512, backward)
        for i in range(2):

            @pl.when(core == 0)
            def _():
                send_back(h, 2, i, 256, right())

            @pl.when(core == 1)
            def _():
                send_back(h, 1, i, 768, left())

    def second_back(h):
        for i in range(2):
            add_back(h, 0, i, backward, pos_mid)

            @pl.when(core == 0)
            def _():
                send_back(h, 1, i, 768, left())

            @pl.when(core == 1)
            def _():
                send_back(h, 2, i, 256, right())

    def third_back(h):
        for i in range(2):
            add_back(h, 1, i, left(), pos_right)
            add_back(h, 2, i, right(), pos_left)
            send_back(h, 3, i, 0, down())

    def fin_swap(h, i, owner=core):
        return remote(fin.at[h, i], dkvh.at[i, heads * owner + h], fin_send.at[h, i], fin_recv.at[h, i], sibling)

    def last_back(h):
        for i in range(2):
            back(h, 3, i, down()).wait_recv()
            whole = acc[h, i, pl.ds(1024, CHIP), :] + rbuf[h, 3, i].astype(jnp.float32)
            if i == 0:
                whole = whole * scale
            whole = whole.astype(jnp.bfloat16)
            for k in (0, 1):

                @pl.when(core == k)
                def _():
                    dkvh[i, heads * k + h] = whole[TOK * k : TOK * (k + 1)]
                    fin[h, i] = whole[TOK * (1 - k) : TOK * (2 - k)]

            fin_swap(h, i).start()

    def dq_swap(h, pair, owner=core):
        return remote(
            dqv.at[pl.ds(group * h + PAIRS * pair, PAIRS)],
            dqh.at[pl.ds(qheads * owner + group * h + PAIRS * pair, PAIRS)],
            dq_send.at[h, pair],
            dq_recv.at[h, pair],
            sibling,
        )

    for h in range(heads):
        send_own(h, 4, up)
        if h < 2:
            own_send(h)
        swap(h).start()
    loads[2].wait()
    loads[3].wait()
    for k in (0, 1):

        @pl.when(core == k)
        def _():
            other = pl.ds(qheads * (1 - k), qheads)
            q_swap[...] = jnp.transpose(q_raw[:, other, :], (1, 0, 2))
            do_swap[...] = jnp.transpose(do_raw[:, other, :], (1, 0, 2))

    for h in range(heads):
        for n in range(2):
            x_swap(n, h).start()
    far_ready(0)
    for k in (0, 1):

        @pl.when(core == k)
        def _():
            mine = pl.ds(qheads * k, qheads)
            qv[k] = jnp.transpose(q_raw[:, mine, :], (1, 0, 2))
            dov[k] = jnp.transpose(do_raw[:, mine, :], (1, 0, 2))
            for h in range(heads):
                kvb[h, :, pl.ds(1024 + TOK * k, TOK), :] = kv_own[:, heads * k + h]

    relay(0)
    own_send(2)

    loads[4].wait()
    start_pos = chip * CHIP
    token = lax.broadcasted_iota(jnp.int32, (8, CHIP), 1) + start_pos

    def doc(number, carry):
        begin, doc_start = carry
        return begin + lengths[number], jnp.where(token >= begin, begin, doc_start)

    _, doc_start = lax.fori_loop(0, lengths.shape[0], doc, (jnp.int32(0), jnp.zeros((8, CHIP), jnp.int32)))
    for t in range(2):
        low = doc_start[0:1, TOK * t : TOK * (t + 1)] - (start_pos + TOK * t) + 1024
        high = lax.broadcasted_iota(jnp.int32, (1, TOK), 1) + 1024
        for tile in range(SPAN // TILE):
            key = lax.broadcasted_iota(jnp.int32, (TILE, TOK), 0) + tile * TILE
            bias[t, pl.ds(tile * TILE, TILE), :] = jnp.where((key >= low) & (key <= high), 0.0, -1e30)

    far_ready(1)
    all_ready(0)

    hooks = {
        1: [lambda: relay(1), lambda: own_send(3), lambda: far_ready(2)],
        2: [lambda: far_ready(3)],
        3: [lambda: relay(2)],
        4: [lambda: finish_head(0), lambda: all_ready(1)],
        5: [lambda: relay(3)],
        7: [lambda: second_back(0)],
        8: [lambda: finish_head(1), lambda: all_ready(2)],
        10: [lambda: third_back(0)],
        11: [lambda: second_back(1)],
        12: [lambda: finish_head(2), lambda: all_ready(3)],
        13: [lambda: last_back(0)],
        14: [lambda: third_back(1)],
        15: [lambda: second_back(2)],
    }

    for step in range(steps):
        for each in hooks.get(step, ()):
            each()
        h = step // (2 * pairs)
        t = step // pairs % 2
        pair = step % pairs
        off = t * TOK
        mine = pl.ds(group * h + PAIRS * pair, PAIRS)
        q = qv[t, mine].reshape(ROWS, TOK)
        do = dov[t, mine].reshape(ROWS, TOK)
        tiles = [pl.ds(tile * TILE, TILE) for tile in range(SPAN // TILE)]
        keys = [pl.ds(off + tile * TILE, TILE) for tile in range(SPAN // TILE)]
        top = jnp.full((8, ROWS), -jnp.inf, jnp.float32)
        for tile, key in zip(tiles, keys):
            score = lax.dot_general(kvb[h, 0, key, :], q, NT, preferred_element_type=jnp.float32)
            score = score + jnp.concatenate([bias[t, tile, :]] * PAIRS, axis=1)
            s_scr[tile, :] = score
            dp_scr[tile, :] = lax.dot_general(kvb[h, 1, key, :], do, NT, preferred_element_type=jnp.float32)
            top = jnp.maximum(top, jnp.max(score.reshape(TILE // 8, 8, ROWS), axis=0))
        factor = scale * LOG2E
        shift = jnp.max(top, axis=0, keepdims=True) * factor
        weight = jnp.zeros((8, ROWS), jnp.float32)
        weighted = jnp.zeros((8, ROWS), jnp.float32)
        for tile in tiles:
            expo = jnp.exp2(s_scr[tile, :] * factor - shift)
            s_scr[tile, :] = expo
            weight = weight + jnp.sum(expo.reshape(TILE // 8, 8, ROWS), axis=0)
            weighted = weighted + jnp.sum((expo * dp_scr[tile, :]).reshape(TILE // 8, 8, ROWS), axis=0)
        inverse = 1.0 / jnp.sum(weight, axis=0, keepdims=True)
        delta = jnp.sum(weighted, axis=0, keepdims=True) * inverse
        for tile, key in zip(tiles, keys):
            prob = s_scr[tile, :] * inverse
            dscore = (prob * (dp_scr[tile, :] - delta)).astype(jnp.bfloat16)
            dsb[tile, :] = dscore
            terms = (
                jnp.dot(dscore, q, preferred_element_type=jnp.float32),
                jnp.dot(prob.astype(jnp.bfloat16), do, preferred_element_type=jnp.float32),
            )
            first = pair == 0 and (t == 0 or key.start >= SPAN)
            for i in range(2):
                acc[h, i, key, :] = terms[i] if first else acc[h, i, key, :] + terms[i]
        dq = lax.dot_general(dsb[...], kvb[h, 0, pl.ds(off, SPAN), :], TN, preferred_element_type=jnp.float32)
        dq = (dq * scale).astype(jnp.bfloat16).reshape(PAIRS, TOK, TOK)

        @pl.when(core == t)
        def _():
            dqh[pl.ds(qheads * t + group * h + PAIRS * pair, PAIRS)] = dq

        @pl.when(core == 1 - t)
        def _():
            dqv[mine] = dq
            dq_swap(h, pair).start()

    finish_head(3)
    last_back(1)
    third_back(2)
    for h in range(heads):
        for pair in range(pairs):
            dq_swap(h, pair).wait_send()
            dq_swap(h, pair, 1 - core).wait_recv()
    for k in (0, 1):
        some = pl.ds(qheads * k, qheads)
        dq_out[:, some, :] = jnp.transpose(dqh[some], (1, 0, 2))
    second_back(3)
    last_back(2)
    third_back(3)
    last_back(3)

    for h in range(heads):
        swap(h).wait_send()
        for slot, target in ((1, right()), (2, onward), (3, left()), (4, up())):
            for half in (0, 1):
                forward(h, slot, 0, half, target).wait_send()
        for n in range(2):
            x_swap(n, h).wait_send()
        for i in range(2):
            for n, target in enumerate((backward, left(), right(), down())):
                back(h, n, i, target).wait_send()
            fin_swap(h, i).wait_send()
            fin_swap(h, i, 1 - core).wait_recv()
    dk_out[...] = jnp.transpose(dkvh[0], (1, 0, 2))
    dv_out[...] = jnp.transpose(dkvh[1], (1, 0, 2))


def put(dq, dk, dv, dq_out, dk_out, dv_out, sem):
    copies = [
        pltpu.make_async_copy(src, dst, sem.at[n])
        for n, (src, dst) in enumerate(((dq, dq_out), (dk, dk_out), (dv, dv_out)))
    ]
    for copy in copies:
        copy.start()
    for copy in copies:
        copy.wait()


def solution(mesh):
    blocks, chips = mesh.shape["ctx"], mesh.shape["uly"] // 2

    def local(queries, keys, values, grad_out, doc_lengths):
        tokens, query_heads, dim = queries.shape
        kv_heads = keys.shape[1]
        heads, group = kv_heads // 2, query_heads // kv_heads
        qheads = heads * group
        pairs = group // PAIRS
        bf16, f32 = jnp.bfloat16, jnp.float32
        vmem, dma = pltpu.VMEM, pltpu.SemaphoreType.DMA
        inside = pl.BlockSpec(memory_space=pltpu.VMEM)
        outside = pl.BlockSpec(memory_space=pltpu.HBM)

        def body(*refs):
            kernel(heads, group, chips, blocks, *refs)

        grads = pl.pallas_call(
            body,
            out_shape=[jax.ShapeDtypeStruct(each.shape, bf16) for each in (queries, keys, values)],
            in_specs=[outside] * 5,
            out_specs=[inside] * 3,
            scratch_shapes=[
                pltpu.SMEM(doc_lengths.shape, jnp.int32),
                vmem(queries.shape, bf16),
                vmem(queries.shape, bf16),
                vmem((2,) + keys.shape, bf16),
                vmem((2, kv_heads, tokens, dim), bf16),
                vmem((qheads, tokens, dim), bf16),
                vmem((qheads, tokens, dim), bf16),
                vmem((query_heads, tokens, dim), bf16),
                vmem((2, kv_heads, tokens, dim), bf16),
                vmem((heads, 2, WINDOW, dim), bf16),
                vmem((2, qheads, tokens, dim), bf16),
                vmem((2, qheads, tokens, dim), bf16),
                vmem((2, SPAN, TOK), f32),
                vmem((SPAN, ROWS), f32),
                vmem((SPAN, ROWS), f32),
                vmem((SPAN, ROWS), bf16),
                vmem((heads, 2, WINDOW, dim), f32),
                vmem((qheads, tokens, dim), bf16),
                vmem((heads, 4, 2, CHIP, dim), bf16),
                vmem((heads, 4, 2, CHIP, dim), bf16),
                vmem((heads, 2, TOK, dim), bf16),
                dma((heads,)),
                dma((heads,)),
                dma((heads, 4, 2)),
                dma((heads, 4, 2)),
                dma((2, heads)),
                dma((2, heads)),
                dma((heads, 4, 2)),
                dma((heads, 4, 2)),
                dma((heads, pairs)),
                dma((heads, pairs)),
                dma((heads, 2)),
                dma((heads, 2)),
                dma((5,)),
            ],
            compiler_params=pltpu.CompilerParams(
                collective_id=0, has_side_effects=True, vmem_limit_bytes=48 << 20
            ),
        )(
            *[
                pltpu.with_memory_space_constraint(each, pltpu.HBM)
                for each in (doc_lengths, queries, grad_out, keys, values)
            ]
        )
        return pl.pallas_call(
            put,
            out_shape=[jax.ShapeDtypeStruct(each.shape, bf16) for each in grads],
            in_specs=[pl.BlockSpec(memory_space=pl.ANY)] * 3,
            out_specs=[outside] * 3,
            scratch_shapes=[dma((3,))],
            compiler_params=pltpu.CompilerParams(vmem_limit_bytes=4 << 20),
        )(*grads)

    spread = P(("ctx", "uly"), None, None)
    return jax.shard_map(
        local,
        mesh=mesh,
        in_specs=(spread, spread, spread, spread, P()),
        out_specs=(spread, spread, spread),
        check_vma=False,
    )
```

```python
import jax
import jax.numpy as jnp
from jax import lax
from jax.experimental import pallas as pl
from jax.experimental.pallas import tpu as pltpu
from jax.sharding import PartitionSpec as P

MESH = pl.DeviceIdType.MESH
NT = (((1,), (1,)), ((), ()))
TN = (((0,), (0,)), ((), ()))
LOG2E = 1.4426950408889634

TOK = 128
CHIP = 256
WINDOW = 1280
SPAN = 1152
TILE = 128
ROWS = 256
PAIRS = ROWS // TOK


def kernel(
    heads,
    group,
    chips,
    blocks,
    lengths_in,
    q_in,
    do_in,
    k_in,
    v_in,
    dq_out,
    dk_out,
    dv_out,
    lengths,
    q_raw,
    do_raw,
    kv_raw,
    kv_own,
    q_swap,
    do_swap,
    dqh,
    dkvh,
    kvb,
    qv,
    dov,
    bias,
    s_scr,
    dp_scr,
    dsb,
    acc,
    dqv,
    sbuf,
    rbuf,
    fin,
    swap_send,
    swap_recv,
    kv_send,
    kv_recv,
    x_send,
    x_recv,
    g_send,
    g_recv,
    dq_send,
    dq_recv,
    fin_send,
    fin_recv,
    in_sem,
):
    ctx = lax.axis_index("ctx")
    uly = lax.axis_index("uly")
    x, core = uly // 2, uly % 2
    qheads = heads * group
    scale = TOK**-0.5
    chip = ctx * chips + x
    total = blocks * chips
    pairs = group // PAIRS
    steps = heads * 2 * pairs

    def at(block, place, its_core):
        return (block % blocks, (place % chips) * 2 + its_core)

    def device(number):
        number = (number + total) % total
        return (number // chips, (number % chips) * 2 + core)

    sibling = (ctx, uly + 1 - 2 * core)

    def up(its_core=core):
        return at(ctx + 1, x, its_core)

    def down(its_core=core):
        return at(ctx + blocks - 1, x, its_core)

    def right(its_core=core):
        return at(ctx, x + 1, its_core)

    def left(its_core=core):
        return at(ctx, x + chips - 1, its_core)

    onward = device(chip + 1 - 2 * core)
    backward = device(chip - 1 + 2 * core)

    pos_right = 1024 * (1 - x // (chips - 1))
    pos_left = 1024 * (1 - (x + chips - 2) // (chips - 1))
    pos_mid = 768 - 512 * core

    sources = (k_in, v_in, q_in, do_in, lengths_in)
    places = (kv_raw.at[0], kv_raw.at[1], q_raw, do_raw, lengths)
    loads = [pltpu.make_async_copy(src, dst, in_sem.at[n]) for n, (src, dst) in enumerate(zip(sources, places))]
    for load in loads:
        load.start()
    for n in range(2):
        loads[n].wait()
        kv_own[n] = jnp.transpose(kv_raw[n], (1, 0, 2))

    barrier = pltpu.get_barrier_semaphore()
    partners = [sibling, onward, backward]
    for its_core in (0, 1):
        partners += [up(its_core), down(its_core), right(its_core), left(its_core)]
    for each in partners:
        pl.semaphore_signal(barrier, inc=1, device_id=each, device_id_type=MESH)
    pl.semaphore_wait(barrier, len(partners))

    def remote(src, dst, send, recv, target):
        return pltpu.make_async_remote_copy(
            src_ref=src, dst_ref=dst, send_sem=send, recv_sem=recv, device_id=target, device_id_type=MESH
        )

    def rows_at(pos, half):
        start = pos + TOK * half
        return pl.ds(start if isinstance(start, int) else pl.multiple_of(start, TOK), TOK)

    def swap(h, half=core):
        return remote(
            kv_own.at[:, heads * (1 - core) + h],
            kvb.at[h, :, rows_at(1024, half), :],
            swap_send.at[h],
            swap_recv.at[h],
            sibling,
        )

    def x_swap(n, h, half=core):
        src, dst = ((q_swap, qv), (do_swap, dov))[n]
        return remote(
            src.at[pl.ds(group * h, group)],
            dst.at[half, pl.ds(group * h, group)],
            x_send.at[n, h],
            x_recv.at[n, h],
            sibling,
        )

    def send_own(h, slot, target):
        for j in (0, 1):
            remote(
                kv_own.at[:, heads * j + h],
                kvb.at[h, :, rows_at(1024 - 256 * slot, core), :],
                kv_send.at[h, slot - 1, j],
                kv_recv.at[h, slot - 1, core],
                target(j),
            ).start()

    def forward(h, slot, pos, half, target):
        return remote(
            kvb.at[h, :, rows_at(pos, half), :],
            kvb.at[h, :, rows_at(1024 - 256 * slot, half), :],
            kv_send.at[h, slot - 1, half],
            kv_recv.at[h, slot - 1, half],
            target,
        )

    def own_send(h):
        @pl.when(x < chips - 1)
        def _():
            send_own(h, 1, right)

        @pl.when(x == 0)
        def _():
            send_own(h, 3, left)

    def far_ready(h):
        for half in (0, 1):
            forward(h, 4, 1024, half, up()).wait_recv()

            @pl.when(x == chips - 1)
            def _():
                forward(h, 1, 0, half, right()).start()

            @pl.when(x > 0)
            def _():
                forward(h, 3, 0, half, left()).start()

    def relay(h):
        for half in (0, 1):

            @pl.when(core == 0)
            def _():
                forward(h, 1, 0, half, right()).wait_recv()

            @pl.when(core == 1)
            def _():
                forward(h, 3, 0, half, left()).wait_recv()

            forward(h, 2, pos_mid, half, onward).start()

    def all_ready(h):
        for half in (0, 1):

            @pl.when(core == 1)
            def _():
                forward(h, 1, 0, half, right()).wait_recv()

            @pl.when(core == 0)
            def _():
                forward(h, 3, 0, half, left()).wait_recv()

            forward(h, 2, 0, half, onward).wait_recv()
        swap(h, 1 - core).wait_recv()
        for n in range(2):
            x_swap(n, h, 1 - core).wait_recv()

    def back(h, n, i, target):
        return remote(sbuf.at[h, n, i], rbuf.at[h, n, i], g_send.at[h, n, i], g_recv.at[h, n, i], target)

    def send_back(h, n, i, pos, target):
        sbuf[h, n, i] = acc[h, i, pl.ds(pos, CHIP), :].astype(jnp.bfloat16)
        back(h, n, i, target).start()

    def add_back(h, n, i, target, pos):
        back(h, n, i, target).wait_recv()
        rows = pl.ds(pl.multiple_of(pos, 256), CHIP)
        acc[h, i, rows, :] = acc[h, i, rows, :] + rbuf[h, n, i].astype(jnp.float32)

    def two_back(h):
        for i in range(2):
            send_back(h, 0, i, 512, backward)

    def one_back(h):
        for i in range(2):

            @pl.when(core == 0)
            def _():
                send_back(h, 2, i, 256, right())

            @pl.when(core == 1)
            def _():
                send_back(h, 1, i, 768, left())

    def finish_head(h):
        two_back(h)
        one_back(h)

    def second_back(h):
        for i in range(2):
            add_back(h, 0, i, backward, pos_mid)

            @pl.when(core == 0)
            def _():
                send_back(h, 1, i, 768, left())

            @pl.when(core == 1)
            def _():
                send_back(h, 2, i, 256, right())

    def third_back(h):
        for i in range(2):
            add_back(h, 1, i, left(), pos_right)
            add_back(h, 2, i, right(), pos_left)
            send_back(h, 3, i, 0, down())

    def fin_swap(h, i, owner=core):
        return remote(fin.at[h, i], dkvh.at[i, heads * owner + h], fin_send.at[h, i], fin_recv.at[h, i], sibling)

    def last_back(h):
        for i in range(2):
            back(h, 3, i, down()).wait_recv()
            whole = acc[h, i, pl.ds(1024, CHIP), :] + rbuf[h, 3, i].astype(jnp.float32)
            if i == 0:
                whole = whole * scale
            whole = whole.astype(jnp.bfloat16)
            for k in (0, 1):

                @pl.when(core == k)
                def _():
                    dkvh[i, heads * k + h] = whole[TOK * k : TOK * (k + 1)]
                    fin[h, i] = whole[TOK * (1 - k) : TOK * (2 - k)]

            fin_swap(h, i).start()

    def dq_swap(h, pair, owner=core):
        return remote(
            dqv.at[pl.ds(group * h + PAIRS * pair, PAIRS)],
            dqh.at[pl.ds(qheads * owner + group * h + PAIRS * pair, PAIRS)],
            dq_send.at[h, pair],
            dq_recv.at[h, pair],
            sibling,
        )

    for h in range(heads):
        send_own(h, 4, up)
        if h < 2:
            own_send(h)
        swap(h).start()
    loads[2].wait()
    loads[3].wait()
    for k in (0, 1):

        @pl.when(core == k)
        def _():
            other = pl.ds(qheads * (1 - k), qheads)
            q_swap[...] = jnp.transpose(q_raw[:, other, :], (1, 0, 2))
            do_swap[...] = jnp.transpose(do_raw[:, other, :], (1, 0, 2))

    for h in range(heads):
        for n in range(2):
            x_swap(n, h).start()
    far_ready(0)
    for k in (0, 1):

        @pl.when(core == k)
        def _():
            mine = pl.ds(qheads * k, qheads)
            qv[k] = jnp.transpose(q_raw[:, mine, :], (1, 0, 2))
            dov[k] = jnp.transpose(do_raw[:, mine, :], (1, 0, 2))
            for h in range(heads):
                kvb[h, :, pl.ds(1024 + TOK * k, TOK), :] = kv_own[:, heads * k + h]

    relay(0)
    own_send(2)

    loads[4].wait()
    start_pos = chip * CHIP
    token = lax.broadcasted_iota(jnp.int32, (8, CHIP), 1) + start_pos

    def doc(number, carry):
        begin, doc_start = carry
        return begin + lengths[number], jnp.where(token >= begin, begin, doc_start)

    _, doc_start = lax.fori_loop(0, lengths.shape[0], doc, (jnp.int32(0), jnp.zeros((8, CHIP), jnp.int32)))
    for t in range(2):
        low = doc_start[0:1, TOK * t : TOK * (t + 1)] - (start_pos + TOK * t) + 1024
        high = lax.broadcasted_iota(jnp.int32, (1, TOK), 1) + 1024
        for tile in range(SPAN // TILE):
            key = lax.broadcasted_iota(jnp.int32, (TILE, TOK), 0) + tile * TILE
            bias[t, pl.ds(tile * TILE, TILE), :] = jnp.where((key >= low) & (key <= high), 0.0, -1e30)

    far_ready(1)
    all_ready(0)

    hooks = {
        1: [lambda: relay(1), lambda: own_send(3), lambda: far_ready(2)],
        2: [lambda: far_ready(3)],
        3: [lambda: relay(2)],
        4: [lambda: finish_head(0), lambda: all_ready(1)],
        5: [lambda: relay(3)],
        7: [lambda: second_back(0)],
        8: [lambda: finish_head(1), lambda: all_ready(2)],
        10: [lambda: third_back(0)],
        11: [lambda: second_back(1)],
        12: [lambda: finish_head(2), lambda: all_ready(3)],
        13: [lambda: last_back(0)],
        14: [lambda: third_back(1)],
        15: [lambda: second_back(2)],
    }

    stats = {}

    def place_of(step):
        return step // (2 * pairs), step // pairs % 2, step % pairs

    def rows_of(step):
        h, t, pair = place_of(step)
        mine = pl.ds(group * h + PAIRS * pair, PAIRS)
        return qv[t, mine].reshape(ROWS, TOK), dov[t, mine].reshape(ROWS, TOK)

    def weigh(step):
        h, t, pair = place_of(step)
        room = step % (2 * pairs)
        q, do = rows_of(step)
        tiles = [pl.ds(tile * TILE, TILE) for tile in range(SPAN // TILE)]
        top = jnp.full((8, ROWS), -jnp.inf, jnp.float32)
        for tile in tiles:
            key = pl.ds(t * TOK + tile.start, TILE)
            score = lax.dot_general(kvb[h, 0, key, :], q, NT, preferred_element_type=jnp.float32)
            score = score + jnp.concatenate([bias[t, tile, :]] * PAIRS, axis=1)
            s_scr[room, tile, :] = score
            dp_scr[room, tile, :] = lax.dot_general(kvb[h, 1, key, :], do, NT, preferred_element_type=jnp.float32)
            top = jnp.maximum(top, jnp.max(score.reshape(TILE // 8, 8, ROWS), axis=0))
        factor = scale * LOG2E
        shift = jnp.max(top, axis=0, keepdims=True) * factor
        weight = jnp.zeros((8, ROWS), jnp.float32)
        weighted = jnp.zeros((8, ROWS), jnp.float32)
        for tile in tiles:
            expo = jnp.exp2(s_scr[room, tile, :] * factor - shift)
            s_scr[room, tile, :] = expo
            weight = weight + jnp.sum(expo.reshape(TILE // 8, 8, ROWS), axis=0)
            weighted = weighted + jnp.sum((expo * dp_scr[room, tile, :]).reshape(TILE // 8, 8, ROWS), axis=0)
        inverse = 1.0 / jnp.sum(weight, axis=0, keepdims=True)
        stats[step] = inverse, jnp.sum(weighted, axis=0, keepdims=True) * inverse

    def spread_terms(step, low=0, high=WINDOW):
        h, t, pair = place_of(step)
        room = step % (2 * pairs)
        q, do = rows_of(step)
        inverse, delta = stats[step]
        for number in range(SPAN // TILE):
            start = t * TOK + number * TILE
            if not low <= start < high:
                continue
            tile, key = pl.ds(number * TILE, TILE), pl.ds(start, TILE)
            prob = s_scr[room, tile, :] * inverse
            dscore = (prob * (dp_scr[room, tile, :] - delta)).astype(jnp.bfloat16)
            dsb[room, tile, :] = dscore
            terms = (
                jnp.dot(dscore, q, preferred_element_type=jnp.float32),
                jnp.dot(prob.astype(jnp.bfloat16), do, preferred_element_type=jnp.float32),
            )
            first = pair == 0 and (t == 0 or start >= SPAN)
            for i in range(2):
                acc[h, i, key, :] = terms[i] if first else acc[h, i, key, :] + terms[i]

    def query_terms(step):
        h, t, pair = place_of(step)
        room = step % (2 * pairs)
        mine = pl.ds(group * h + PAIRS * pair, PAIRS)
        keys = kvb[h, 0, pl.ds(t * TOK, SPAN), :]
        dq = lax.dot_general(dsb[room], keys, TN, preferred_element_type=jnp.float32)
        dq = (dq * scale).astype(jnp.bfloat16).reshape(PAIRS, TOK, TOK)

        @pl.when(core == t)
        def _():
            dqh[pl.ds(qheads * t + group * h + PAIRS * pair, PAIRS)] = dq

        @pl.when(core == 1 - t)
        def _():
            dqv[mine] = dq
            dq_swap(h, pair).start()

    last = range(steps - 2 * pairs, steps)
    for step in range(steps):
        for each in hooks.get(step, ()):
            each()
        weigh(step)
        if step not in last:
            spread_terms(step)
            query_terms(step)

    def chunk_terms(pos):
        for step in last:
            spread_terms(step, pos, pos + CHIP)

    chunk_terms(512)
    two_back(3)
    chunk_terms(256)
    chunk_terms(768)
    one_back(3)
    last_back(1)
    chunk_terms(0)
    third_back(2)
    chunk_terms(1024)
    second_back(3)
    for step in last:
        query_terms(step)
    last_back(2)
    third_back(3)
    for h in range(heads):
        for pair in range(pairs):
            dq_swap(h, pair).wait_send()
            dq_swap(h, pair, 1 - core).wait_recv()
    for k in (0, 1):
        some = pl.ds(qheads * k, qheads)
        dq_out[:, some, :] = jnp.transpose(dqh[some], (1, 0, 2))
    last_back(3)

    for h in range(heads):
        swap(h).wait_send()
        for slot, target in ((1, right()), (2, onward), (3, left()), (4, up())):
            for half in (0, 1):
                forward(h, slot, 0, half, target).wait_send()
        for n in range(2):
            x_swap(n, h).wait_send()
        for i in range(2):
            for n, target in enumerate((backward, left(), right(), down())):
                back(h, n, i, target).wait_send()
            fin_swap(h, i).wait_send()
            fin_swap(h, i, 1 - core).wait_recv()
    dk_out[...] = jnp.transpose(dkvh[0], (1, 0, 2))
    dv_out[...] = jnp.transpose(dkvh[1], (1, 0, 2))


def put(dq, dk, dv, dq_out, dk_out, dv_out, sem):
    copies = [
        pltpu.make_async_copy(src, dst, sem.at[n])
        for n, (src, dst) in enumerate(((dq, dq_out), (dk, dk_out), (dv, dv_out)))
    ]
    for copy in copies:
        copy.start()
    for copy in copies:
        copy.wait()


def solution(mesh):
    blocks, chips = mesh.shape["ctx"], mesh.shape["uly"] // 2

    def local(queries, keys, values, grad_out, doc_lengths):
        tokens, query_heads, dim = queries.shape
        kv_heads = keys.shape[1]
        heads, group = kv_heads // 2, query_heads // kv_heads
        qheads = heads * group
        pairs = group // PAIRS
        bf16, f32 = jnp.bfloat16, jnp.float32
        vmem, dma = pltpu.VMEM, pltpu.SemaphoreType.DMA
        inside = pl.BlockSpec(memory_space=pltpu.VMEM)
        outside = pl.BlockSpec(memory_space=pltpu.HBM)

        def body(*refs):
            kernel(heads, group, chips, blocks, *refs)

        grads = pl.pallas_call(
            body,
            out_shape=[jax.ShapeDtypeStruct(each.shape, bf16) for each in (queries, keys, values)],
            in_specs=[outside] * 5,
            out_specs=[inside] * 3,
            scratch_shapes=[
                pltpu.SMEM(doc_lengths.shape, jnp.int32),
                vmem(queries.shape, bf16),
                vmem(queries.shape, bf16),
                vmem((2,) + keys.shape, bf16),
                vmem((2, kv_heads, tokens, dim), bf16),
                vmem((qheads, tokens, dim), bf16),
                vmem((qheads, tokens, dim), bf16),
                vmem((query_heads, tokens, dim), bf16),
                vmem((2, kv_heads, tokens, dim), bf16),
                vmem((heads, 2, WINDOW, dim), bf16),
                vmem((2, qheads, tokens, dim), bf16),
                vmem((2, qheads, tokens, dim), bf16),
                vmem((2, SPAN, TOK), f32),
                vmem((2 * pairs, SPAN, ROWS), f32),
                vmem((2 * pairs, SPAN, ROWS), f32),
                vmem((2 * pairs, SPAN, ROWS), bf16),
                vmem((heads, 2, WINDOW, dim), f32),
                vmem((qheads, tokens, dim), bf16),
                vmem((heads, 4, 2, CHIP, dim), bf16),
                vmem((heads, 4, 2, CHIP, dim), bf16),
                vmem((heads, 2, TOK, dim), bf16),
                dma((heads,)),
                dma((heads,)),
                dma((heads, 4, 2)),
                dma((heads, 4, 2)),
                dma((2, heads)),
                dma((2, heads)),
                dma((heads, 4, 2)),
                dma((heads, 4, 2)),
                dma((heads, pairs)),
                dma((heads, pairs)),
                dma((heads, 2)),
                dma((heads, 2)),
                dma((5,)),
            ],
            compiler_params=pltpu.CompilerParams(
                collective_id=0, has_side_effects=True, vmem_limit_bytes=48 << 20
            ),
        )(
            *[
                pltpu.with_memory_space_constraint(each, pltpu.HBM)
                for each in (doc_lengths, queries, grad_out, keys, values)
            ]
        )
        return pl.pallas_call(
            put,
            out_shape=[jax.ShapeDtypeStruct(each.shape, bf16) for each in grads],
            in_specs=[pl.BlockSpec(memory_space=pl.ANY)] * 3,
            out_specs=[outside] * 3,
            scratch_shapes=[dma((3,))],
            compiler_params=pltpu.CompilerParams(vmem_limit_bytes=4 << 20),
        )(*grads)

    spread = P(("ctx", "uly"), None, None)
    return jax.shard_map(
        local,
        mesh=mesh,
        in_specs=(spread, spread, spread, spread, P()),
        out_specs=(spread, spread, spread),
        check_vma=False,
    )
```

```python
import jax
import jax.numpy as jnp
from jax import lax
from jax.experimental import pallas as pl
from jax.experimental.pallas import tpu as pltpu
from jax.sharding import PartitionSpec as P

MESH = pl.DeviceIdType.MESH
NT = (((1,), (1,)), ((), ()))
TN = (((0,), (0,)), ((), ()))
LOG2E = 1.4426950408889634

TOK = 128
CHIP = 256
WINDOW = 1280
SPAN = 1152
TILE = 128
ROWS = 256
PAIRS = ROWS // TOK


def kernel(
    heads,
    group,
    chips,
    blocks,
    lengths_in,
    q_in,
    do_in,
    k_in,
    v_in,
    dq_out,
    dk_out,
    dv_out,
    lengths,
    q_raw,
    do_raw,
    kv_raw,
    kv_own,
    q_swap,
    do_swap,
    dqh,
    dkvh,
    kvb,
    qv,
    dov,
    bias,
    s_scr,
    dp_scr,
    dsb,
    acc,
    dqv,
    sbuf,
    rbuf,
    fin,
    swap_send,
    swap_recv,
    kv_send,
    kv_recv,
    x_send,
    x_recv,
    g_send,
    g_recv,
    dq_send,
    dq_recv,
    fin_send,
    fin_recv,
    in_sem,
):
    ctx = lax.axis_index("ctx")
    uly = lax.axis_index("uly")
    x, core = uly // 2, uly % 2
    qheads = heads * group
    scale = TOK**-0.5
    chip = ctx * chips + x
    total = blocks * chips
    pairs = group // PAIRS
    steps = heads * 2 * pairs

    def at(block, place, its_core):
        return (block % blocks, (place % chips) * 2 + its_core)

    def device(number):
        number = (number + total) % total
        return (number // chips, (number % chips) * 2 + core)

    sibling = (ctx, uly + 1 - 2 * core)

    def up(its_core=core):
        return at(ctx + 1, x, its_core)

    def down(its_core=core):
        return at(ctx + blocks - 1, x, its_core)

    def right(its_core=core):
        return at(ctx, x + 1, its_core)

    def left(its_core=core):
        return at(ctx, x + chips - 1, its_core)

    onward = device(chip + 1 - 2 * core)
    backward = device(chip - 1 + 2 * core)

    pos_right = 1024 * (1 - x // (chips - 1))
    pos_left = 1024 * (1 - (x + chips - 2) // (chips - 1))
    pos_mid = 768 - 512 * core

    sources = (k_in, v_in, q_in, do_in, lengths_in)
    places = (kv_raw.at[0], kv_raw.at[1], q_raw, do_raw, lengths)
    loads = [pltpu.make_async_copy(src, dst, in_sem.at[n]) for n, (src, dst) in enumerate(zip(sources, places))]
    for load in loads:
        load.start()
    for n in range(2):
        loads[n].wait()
        kv_own[n] = jnp.transpose(kv_raw[n], (1, 0, 2))

    barrier = pltpu.get_barrier_semaphore()
    partners = [sibling, onward, backward]
    for its_core in (0, 1):
        partners += [up(its_core), down(its_core), right(its_core), left(its_core)]
    for each in partners:
        pl.semaphore_signal(barrier, inc=1, device_id=each, device_id_type=MESH)
    pl.semaphore_wait(barrier, len(partners))

    def remote(src, dst, send, recv, target):
        return pltpu.make_async_remote_copy(
            src_ref=src, dst_ref=dst, send_sem=send, recv_sem=recv, device_id=target, device_id_type=MESH
        )

    def rows_at(pos, half):
        start = pos + TOK * half
        return pl.ds(start if isinstance(start, int) else pl.multiple_of(start, TOK), TOK)

    def swap(h, half=core):
        return remote(
            kv_own.at[:, heads * (1 - core) + h],
            kvb.at[h, :, rows_at(1024, half), :],
            swap_send.at[h],
            swap_recv.at[h],
            sibling,
        )

    def x_swap(n, h, half=core):
        src, dst = ((q_swap, qv), (do_swap, dov))[n]
        return remote(
            src.at[pl.ds(group * h, group)],
            dst.at[half, pl.ds(group * h, group)],
            x_send.at[n, h],
            x_recv.at[n, h],
            sibling,
        )

    def send_own(h, slot, target):
        for j in (0, 1):
            remote(
                kv_own.at[:, heads * j + h],
                kvb.at[h, :, rows_at(1024 - 256 * slot, core), :],
                kv_send.at[h, slot - 1, j],
                kv_recv.at[h, slot - 1, core],
                target(j),
            ).start()

    def forward(h, slot, pos, half, target):
        return remote(
            kvb.at[h, :, rows_at(pos, half), :],
            kvb.at[h, :, rows_at(1024 - 256 * slot, half), :],
            kv_send.at[h, slot - 1, half],
            kv_recv.at[h, slot - 1, half],
            target,
        )

    def own_send(h):
        @pl.when(x < chips - 1)
        def _():
            send_own(h, 1, right)

        @pl.when(x == 0)
        def _():
            send_own(h, 3, left)

    def far_ready(h):
        for half in (0, 1):
            forward(h, 4, 1024, half, up()).wait_recv()

            @pl.when(x == chips - 1)
            def _():
                forward(h, 1, 0, half, right()).start()

            @pl.when(x > 0)
            def _():
                forward(h, 3, 0, half, left()).start()

    def relay(h):
        for half in (0, 1):

            @pl.when(core == 0)
            def _():
                forward(h, 1, 0, half, right()).wait_recv()

            @pl.when(core == 1)
            def _():
                forward(h, 3, 0, half, left()).wait_recv()

            forward(h, 2, pos_mid, half, onward).start()

    def all_ready(h):
        for half in (0, 1):

            @pl.when(core == 1)
            def _():
                forward(h, 1, 0, half, right()).wait_recv()

            @pl.when(core == 0)
            def _():
                forward(h, 3, 0, half, left()).wait_recv()

            forward(h, 2, 0, half, onward).wait_recv()
        swap(h, 1 - core).wait_recv()
        for n in range(2):
            x_swap(n, h, 1 - core).wait_recv()

    def back(h, n, i, target):
        return remote(sbuf.at[h, n, i], rbuf.at[h, n, i], g_send.at[h, n, i], g_recv.at[h, n, i], target)

    def send_back(h, n, i, pos, target):
        sbuf[h, n, i] = acc[h, i, pl.ds(pos, CHIP), :].astype(jnp.bfloat16)
        back(h, n, i, target).start()

    def add_back(h, n, i, target, pos):
        back(h, n, i, target).wait_recv()
        rows = pl.ds(pl.multiple_of(pos, 256), CHIP)
        acc[h, i, rows, :] = acc[h, i, rows, :] + rbuf[h, n, i].astype(jnp.float32)

    def two_back(h):
        for i in range(2):
            send_back(h, 0, i, 512, backward)

    def one_back(h):
        for i in range(2):

            @pl.when(core == 0)
            def _():
                send_back(h, 2, i, 256, right())

            @pl.when(core == 1)
            def _():
                send_back(h, 1, i, 768, left())

    def finish_head(h):
        two_back(h)
        one_back(h)

    def second_back(h):
        for i in range(2):
            add_back(h, 0, i, backward, pos_mid)

            @pl.when(core == 0)
            def _():
                send_back(h, 1, i, 768, left())

            @pl.when(core == 1)
            def _():
                send_back(h, 2, i, 256, right())

    def third_back(h):
        for i in range(2):
            add_back(h, 1, i, left(), pos_right)
            add_back(h, 2, i, right(), pos_left)
            send_back(h, 3, i, 0, down())

    def fin_swap(h, i, owner=core):
        return remote(fin.at[h, i], dkvh.at[i, heads * owner + h], fin_send.at[h, i], fin_recv.at[h, i], sibling)

    def last_back(h):
        for i in range(2):
            back(h, 3, i, down()).wait_recv()
            whole = acc[h, i, pl.ds(1024, CHIP), :] + rbuf[h, 3, i].astype(jnp.float32)
            if i == 0:
                whole = whole * scale
            whole = whole.astype(jnp.bfloat16)
            for k in (0, 1):

                @pl.when(core == k)
                def _():
                    dkvh[i, heads * k + h] = whole[TOK * k : TOK * (k + 1)]
                    fin[h, i] = whole[TOK * (1 - k) : TOK * (2 - k)]

            fin_swap(h, i).start()

    def dq_swap(h, pair, owner=core):
        return remote(
            dqv.at[pl.ds(group * h + PAIRS * pair, PAIRS)],
            dqh.at[pl.ds(qheads * owner + group * h + PAIRS * pair, PAIRS)],
            dq_send.at[h, pair],
            dq_recv.at[h, pair],
            sibling,
        )

    for h in range(heads):
        send_own(h, 4, up)
        if h < 2:
            own_send(h)
        swap(h).start()
    loads[2].wait()
    loads[3].wait()
    for k in (0, 1):

        @pl.when(core == k)
        def _():
            other = pl.ds(qheads * (1 - k), qheads)
            q_swap[...] = jnp.transpose(q_raw[:, other, :], (1, 0, 2))
            do_swap[...] = jnp.transpose(do_raw[:, other, :], (1, 0, 2))

    for h in range(heads):
        for n in range(2):
            x_swap(n, h).start()
    far_ready(0)
    for k in (0, 1):

        @pl.when(core == k)
        def _():
            mine = pl.ds(qheads * k, qheads)
            qv[k] = jnp.transpose(q_raw[:, mine, :], (1, 0, 2))
            dov[k] = jnp.transpose(do_raw[:, mine, :], (1, 0, 2))
            for h in range(heads):
                kvb[h, :, pl.ds(1024 + TOK * k, TOK), :] = kv_own[:, heads * k + h]

    relay(0)
    own_send(2)

    loads[4].wait()
    start_pos = chip * CHIP
    token = lax.broadcasted_iota(jnp.int32, (8, CHIP), 1) + start_pos

    def doc(number, carry):
        begin, doc_start = carry
        return begin + lengths[number], jnp.where(token >= begin, begin, doc_start)

    _, doc_start = lax.fori_loop(0, lengths.shape[0], doc, (jnp.int32(0), jnp.zeros((8, CHIP), jnp.int32)))
    for t in range(2):
        low = doc_start[0:1, TOK * t : TOK * (t + 1)] - (start_pos + TOK * t) + 1024
        high = lax.broadcasted_iota(jnp.int32, (1, TOK), 1) + 1024
        for tile in range(SPAN // TILE):
            key = lax.broadcasted_iota(jnp.int32, (TILE, TOK), 0) + tile * TILE
            bias[t, pl.ds(tile * TILE, TILE), :] = jnp.where((key >= low) & (key <= high), 0.0, -1e30)

    far_ready(1)
    all_ready(0)

    hooks = {
        1: [lambda: relay(1), lambda: own_send(3), lambda: far_ready(2)],
        2: [lambda: far_ready(3)],
        3: [lambda: relay(2)],
        4: [lambda: finish_head(0), lambda: all_ready(1)],
        5: [lambda: relay(3)],
        7: [lambda: second_back(0)],
        8: [lambda: finish_head(1), lambda: all_ready(2)],
        10: [lambda: third_back(0)],
        11: [lambda: second_back(1)],
        12: [lambda: finish_head(2), lambda: all_ready(3)],
        14: [lambda: last_back(0)],
        15: [lambda: third_back(1)],
    }

    stats = {}

    def place_of(step):
        return step // (2 * pairs), step // pairs % 2, step % pairs

    def rows_of(step):
        h, t, pair = place_of(step)
        mine = pl.ds(group * h + PAIRS * pair, PAIRS)
        return qv[t, mine].reshape(ROWS, TOK), dov[t, mine].reshape(ROWS, TOK)

    def weigh(step):
        h, t, pair = place_of(step)
        room = step % (2 * pairs)
        q, do = rows_of(step)
        tiles = [pl.ds(tile * TILE, TILE) for tile in range(SPAN // TILE)]
        top = jnp.full((8, ROWS), -jnp.inf, jnp.float32)
        for tile in tiles:
            key = pl.ds(t * TOK + tile.start, TILE)
            score = lax.dot_general(kvb[h, 0, key, :], q, NT, preferred_element_type=jnp.float32)
            score = score + jnp.concatenate([bias[t, tile, :]] * PAIRS, axis=1)
            s_scr[room, tile, :] = score
            dp_scr[room, tile, :] = lax.dot_general(kvb[h, 1, key, :], do, NT, preferred_element_type=jnp.float32)
            top = jnp.maximum(top, jnp.max(score.reshape(TILE // 8, 8, ROWS), axis=0))
        factor = scale * LOG2E
        shift = jnp.max(top, axis=0, keepdims=True) * factor
        weight = jnp.zeros((8, ROWS), jnp.float32)
        weighted = jnp.zeros((8, ROWS), jnp.float32)
        for tile in tiles:
            expo = jnp.exp2(s_scr[room, tile, :] * factor - shift)
            s_scr[room, tile, :] = expo
            weight = weight + jnp.sum(expo.reshape(TILE // 8, 8, ROWS), axis=0)
            weighted = weighted + jnp.sum((expo * dp_scr[room, tile, :]).reshape(TILE // 8, 8, ROWS), axis=0)
        inverse = 1.0 / jnp.sum(weight, axis=0, keepdims=True)
        stats[step] = inverse, jnp.sum(weighted, axis=0, keepdims=True) * inverse

    def spread_terms(step, low=0, high=WINDOW):
        h, t, pair = place_of(step)
        room = step % (2 * pairs)
        q, do = rows_of(step)
        inverse, delta = stats[step]
        for number in range(SPAN // TILE):
            start = t * TOK + number * TILE
            if not low <= start < high:
                continue
            tile, key = pl.ds(number * TILE, TILE), pl.ds(start, TILE)
            prob = s_scr[room, tile, :] * inverse
            dscore = (prob * (dp_scr[room, tile, :] - delta)).astype(jnp.bfloat16)
            dsb[room, tile, :] = dscore
            terms = (
                jnp.dot(dscore, q, preferred_element_type=jnp.float32),
                jnp.dot(prob.astype(jnp.bfloat16), do, preferred_element_type=jnp.float32),
            )
            first = pair == 0 and (t == 0 or start >= SPAN)
            for i in range(2):
                acc[h, i, key, :] = terms[i] if first else acc[h, i, key, :] + terms[i]

    def query_terms(step):
        h, t, pair = place_of(step)
        room = step % (2 * pairs)
        mine = pl.ds(group * h + PAIRS * pair, PAIRS)
        keys = kvb[h, 0, pl.ds(t * TOK, SPAN), :]
        dq = lax.dot_general(dsb[room], keys, TN, preferred_element_type=jnp.float32)
        dq = (dq * scale).astype(jnp.bfloat16).reshape(PAIRS, TOK, TOK)

        @pl.when(core == t)
        def _():
            dqh[pl.ds(qheads * t + group * h + PAIRS * pair, PAIRS)] = dq

        @pl.when(core == 1 - t)
        def _():
            dqv[mine] = dq
            dq_swap(h, pair).start()

    last = range(steps - 2 * pairs, steps)
    for step in range(steps):
        for each in hooks.get(step, ()):
            each()
        weigh(step)
        if step not in last:
            spread_terms(step)
            query_terms(step)

    def chunk_terms(pos):
        for step in last:
            spread_terms(step, pos, pos + CHIP)

    chunk_terms(512)
    two_back(3)
    second_back(2)
    chunk_terms(256)
    chunk_terms(768)
    one_back(3)
    chunk_terms(0)
    last_back(1)
    chunk_terms(1024)
    third_back(2)
    second_back(3)
    for step in last:
        query_terms(step)
    last_back(2)
    third_back(3)
    for h in range(heads):
        for pair in range(pairs):
            dq_swap(h, pair).wait_send()
            dq_swap(h, pair, 1 - core).wait_recv()
    for k in (0, 1):
        some = pl.ds(qheads * k, qheads)
        dq_out[:, some, :] = jnp.transpose(dqh[some], (1, 0, 2))
    last_back(3)

    for h in range(heads):
        swap(h).wait_send()
        for slot, target in ((1, right()), (2, onward), (3, left()), (4, up())):
            for half in (0, 1):
                forward(h, slot, 0, half, target).wait_send()
        for n in range(2):
            x_swap(n, h).wait_send()
        for i in range(2):
            for n, target in enumerate((backward, left(), right(), down())):
                back(h, n, i, target).wait_send()
            fin_swap(h, i).wait_send()
            fin_swap(h, i, 1 - core).wait_recv()
    dk_out[...] = jnp.transpose(dkvh[0], (1, 0, 2))
    dv_out[...] = jnp.transpose(dkvh[1], (1, 0, 2))


def put(dq, dk, dv, dq_out, dk_out, dv_out, sem):
    copies = [
        pltpu.make_async_copy(src, dst, sem.at[n])
        for n, (src, dst) in enumerate(((dq, dq_out), (dk, dk_out), (dv, dv_out)))
    ]
    for copy in copies:
        copy.start()
    for copy in copies:
        copy.wait()


def solution(mesh):
    blocks, chips = mesh.shape["ctx"], mesh.shape["uly"] // 2

    def local(queries, keys, values, grad_out, doc_lengths):
        tokens, query_heads, dim = queries.shape
        kv_heads = keys.shape[1]
        heads, group = kv_heads // 2, query_heads // kv_heads
        qheads = heads * group
        pairs = group // PAIRS
        bf16, f32 = jnp.bfloat16, jnp.float32
        vmem, dma = pltpu.VMEM, pltpu.SemaphoreType.DMA
        inside = pl.BlockSpec(memory_space=pltpu.VMEM)
        outside = pl.BlockSpec(memory_space=pltpu.HBM)

        def body(*refs):
            kernel(heads, group, chips, blocks, *refs)

        grads = pl.pallas_call(
            body,
            out_shape=[jax.ShapeDtypeStruct(each.shape, bf16) for each in (queries, keys, values)],
            in_specs=[outside] * 5,
            out_specs=[inside] * 3,
            scratch_shapes=[
                pltpu.SMEM(doc_lengths.shape, jnp.int32),
                vmem(queries.shape, bf16),
                vmem(queries.shape, bf16),
                vmem((2,) + keys.shape, bf16),
                vmem((2, kv_heads, tokens, dim), bf16),
                vmem((qheads, tokens, dim), bf16),
                vmem((qheads, tokens, dim), bf16),
                vmem((query_heads, tokens, dim), bf16),
                vmem((2, kv_heads, tokens, dim), bf16),
                vmem((heads, 2, WINDOW, dim), bf16),
                vmem((2, qheads, tokens, dim), bf16),
                vmem((2, qheads, tokens, dim), bf16),
                vmem((2, SPAN, TOK), f32),
                vmem((2 * pairs, SPAN, ROWS), f32),
                vmem((2 * pairs, SPAN, ROWS), f32),
                vmem((2 * pairs, SPAN, ROWS), bf16),
                vmem((heads, 2, WINDOW, dim), f32),
                vmem((qheads, tokens, dim), bf16),
                vmem((heads, 4, 2, CHIP, dim), bf16),
                vmem((heads, 4, 2, CHIP, dim), bf16),
                vmem((heads, 2, TOK, dim), bf16),
                dma((heads,)),
                dma((heads,)),
                dma((heads, 4, 2)),
                dma((heads, 4, 2)),
                dma((2, heads)),
                dma((2, heads)),
                dma((heads, 4, 2)),
                dma((heads, 4, 2)),
                dma((heads, pairs)),
                dma((heads, pairs)),
                dma((heads, 2)),
                dma((heads, 2)),
                dma((5,)),
            ],
            compiler_params=pltpu.CompilerParams(
                collective_id=0, has_side_effects=True, vmem_limit_bytes=48 << 20
            ),
        )(
            *[
                pltpu.with_memory_space_constraint(each, pltpu.HBM)
                for each in (doc_lengths, queries, grad_out, keys, values)
            ]
        )
        return pl.pallas_call(
            put,
            out_shape=[jax.ShapeDtypeStruct(each.shape, bf16) for each in grads],
            in_specs=[pl.BlockSpec(memory_space=pl.ANY)] * 3,
            out_specs=[outside] * 3,
            scratch_shapes=[dma((3,))],
            compiler_params=pltpu.CompilerParams(vmem_limit_bytes=4 << 20),
        )(*grads)

    spread = P(("ctx", "uly"), None, None)
    return jax.shard_map(
        local,
        mesh=mesh,
        in_specs=(spread, spread, spread, spread, P()),
        out_specs=(spread, spread, spread),
        check_vma=False,
    )
```
